32 devices in a mesh: seq: 8 (over z, y), head: 4 (over x, core).
Axes of the slice: x: 2, y: 2, z: 4, core: 2. Of those that a mesh axis runs over, the one named last changes fastest.
Arguments:
- tokens: bfloat16 [4096, 3072], P(('seq', 'head')), may hold values from -6 to 6
- owner_shard: int32 [4096, 1], P(('seq', 'head')), may hold values from 0 to 7; in each aligned block of 128 rows (0 to 127, 128 to 255, ...) at most 48 rows name the same one
- dest_slot: int32 [4096], P(('seq', 'head')), may hold values from 0 to 127
- w_qkv: bfloat16 [3072, 3, 1536], P(None, None, 'head'), may hold values from -0.109375 to 0.109375
- w_out: bfloat16 [1536, 3072], P('head'), may hold values from -3 to 3
- norm_gain: float32 [3072], replicated, may hold values from 0.5 to 1.5
- norm_shift: float32 [3072], replicated, may hold values from -3 to 3
- query_gain: float32 [128], replicated, may hold values from 0.5 to 16
- key_gain: float32 [128], replicated, may hold values from 0.5 to 16
- out_gate: float32 [3072], replicated, may hold values from 0.5 to 2
Outputs:
- unmerged: bfloat16 [4096, 3072], P(('seq', 'head'))
The draws below stay inside these ranges and needn't reach their ends.
Inputs may be any that keep to these rules, and one draw needn't show every extreme that they name: `owner_shard`: among the rows of one device at most 48 name the same owner, a bound that some block reaches of them on some or all devices.
All inputs are finite; a program needn't handle non-finite values.
Results may differ from the reference program's by a relative error of at most 0.01195.
The reference program's roundings to bfloat16 on the way (of `normed`, `queries`, `keys_all`, `values_all`, `expweights`, `attended` and `merged_out`) count: a program that leaves them out, or rounds other values in their place, can miss the bound.
Values may be sent and summed in bfloat16 or wider, within the bound.
A program may use at most 128 MiB of HBM per device.

```python
import math
import jax
import jax.numpy as jnp
import numpy as np
from jax import lax

D = 3072
HDIM = 128
SRC_DEV = 128
HEADS = 12
TOKENS = 4096
MRG_SEQ = 128
MERGED = 1024
CAP = 48
N_SEQ = 8


def spread_gain(key, salt_number):
    lower_end = math.log(0.5)
    upper_end = math.log(2.0)
    baseline = jnp.exp(jax.random.uniform(jax.random.fold_in(key, salt_number), (HDIM,), jnp.float32, lower_end, upper_end))
    return baseline


def draw_query_gain(key, part):
    return spread_gain(key, 11)


def draw_key_gain(key, part):
    return spread_gain(key, 23)


def place_ends(array, own_key, smallest, high):
    spot = [jax.random.randint(jax.random.fold_in(own_key, axis), (), 0, length) for axis, length in enumerate(array.shape)]
    longest = array.shape.index(max(array.shape))
    beside = spot[:longest] + [(spot[longest] + 1) % array.shape[longest]] + spot[longest + 1:]
    return array.at[tuple(spot)].set(smallest).at[tuple(beside)].set(high)


def levels(rng, dims, shards, least, top_value):
    def one(dim, blocks):
        heights = jax.random.uniform(jax.random.fold_in(jax.random.fold_in(rng, 6), dim), (blocks,), jnp.float32, least / len(shards), top_value / len(shards))
        return jnp.repeat(jnp.exp(heights), dims[dim] // blocks).reshape((-1,) + (1,) * (len(dims) - dim - 1))

    loudness = one(*shards[0])
    for cut in shards[1:]:
        loudness = loudness * one(*cut)
    return loudness


def routed_block(key, own, number, rows, count, top, most, lean):
    order = jax.random.permutation(key, count)
    crowded, usual = load_shares(count, rows * top, most, lean, True), load_shares(count, rows * top, most, lean, False)
    places = jnp.arange(count)

    def named(lengths, offset_by):
        used = int((lengths > 0).sum())
        fixed = max(1, used // 4)
        shifted = fixed + (places - fixed + offset_by * (used - fixed)) % max(1, count - fixed)
        return jnp.zeros((count,), jnp.int32).at[order[jnp.where(places < fixed, places, shifted)]].set(jnp.asarray(lengths, jnp.int32))

    lengths = jnp.where(number % 4 == 0, named(crowded, number // 4), named(usual, number - number // 4 - 1))
    mixed = jax.random.permutation(jax.random.fold_in(own, 3), count)
    giver, taker = mixed[0:count // 2 * 2:2], mixed[1:count // 2 * 2:2]
    room = jnp.minimum(lengths[giver] - 1, most - lengths[taker]) // 2
    room = jnp.where((giver == order[0]) | (taker == order[0]) | (lengths[taker] == 0), 0, jnp.maximum(room, 0))
    shifted = jax.random.randint(jax.random.fold_in(own, 4), (count // 2,), 0, 1 << 20) % (room + 1)
    lengths = lengths.at[giver].add(-shifted).at[taker].add(shifted)
    labels = jnp.searchsorted(jnp.cumsum(lengths), jnp.arange(rows * top), side="right").astype(jnp.int32)
    grid = labels.reshape(top, rows).T
    grid = grid[jax.random.permutation(jax.random.fold_in(own, 1), rows)]
    offset_by = jax.random.randint(jax.random.fold_in(own, 2), (rows, 1), 0, top)
    return jnp.take_along_axis(grid, (jnp.arange(top)[None, :] + offset_by) % top, axis=1)


def load_shares(amount, total, reach, lean, full):
    weights = [(1 << 20) // math.isqrt(grade ** lean) + 1 for grade in range(1, amount + 1)]
    largest = reach if full else min(reach, max(-(-total // amount), total * weights[0] // sum(weights)))
    least = 1 if total - largest >= amount - 1 else 0
    counts, spare = [largest] + [least] * (amount - 1), total - largest - least * (amount - 1)
    while spare > 0:
        candidates = [i for i in range(1, amount) if counts[i] < largest] or [i for i in range(1, amount) if counts[i] < reach]
        pool, budget = sum([weights[i] for i in candidates]), spare
        for i in candidates:
            more = min(reach - counts[i], max(1, budget * weights[i] // pool), spare)
            counts[i] = counts[i] + more
            spare = spare - more
    return np.array(counts)


def scatter_about(key, dims, scale, bound, split=(), dtype=jnp.bfloat16):
    entries = jax.random.normal(key, dims, jnp.float32) * scale
    if len(split) > 0:
        entries = levels(key, dims, split, -0.22, 0.18) * entries
    return jnp.clip(entries, min=-bound, max=bound).astype(dtype)


def setup_inputs(seed: int = 0) -> dict:
    key_of = jax.random.split(jax.random.key(seed), 11)
    tokens = scatter_about(key_of[0], (TOKENS, D), 1.0, 6.0, ((0, 32),))
    owner_shard_keys = jax.random.split(jax.random.fold_in(key_of[1], 1), TOKENS // SRC_DEV)
    owner_shard_turns = jax.random.permutation(jax.random.fold_in(key_of[1], 3), TOKENS // SRC_DEV)
    owner_shard = jax.vmap(lambda own, number: routed_block(jax.random.fold_in(key_of[1], 2), own, number, SRC_DEV, N_SEQ, 1, CAP, 2))(owner_shard_keys, owner_shard_turns).reshape((TOKENS, 1))
    dest_slot = place_ends(jax.random.randint(key_of[2], (TOKENS,), 0, MRG_SEQ), jax.random.fold_in(key_of[2], 1), 0, MRG_SEQ - 1).astype(jnp.int32)
    w_qkv = scatter_about(key_of[3], (D, 3, HEADS * HDIM), D ** -0.5, 0.109375, ((2, 4),))
    w_out = scatter_about(key_of[4], (HEADS * HDIM, D), 0.5, 3.0, ((0, 4),))
    norm_gain = jnp.clip(jax.random.uniform(key_of[5], (D,), jnp.float32, 0.5, 1.5), 0.5, 1.5)
    norm_shift = scatter_about(key_of[6], (D,), 0.5, 3.0, (), jnp.float32)
    query_gain = draw_query_gain(jax.random.fold_in(key_of[10], 71), 0)
    key_gain = draw_key_gain(jax.random.fold_in(key_of[10], 71), 0)
    out_gate = jnp.clip(jax.random.uniform(key_of[9], (D,), jnp.float32, 0.5, 2.0), 0.5, 2.0)
    return {"tokens": tokens, "owner_shard": owner_shard, "dest_slot": dest_slot, "w_qkv": w_qkv, "w_out": w_out, "norm_gain": norm_gain, "norm_shift": norm_shift, "query_gain": query_gain, "key_gain": key_gain, "out_gate": out_gate}


def rms_scale(values_in):
    return values_in * lax.rsqrt(lax.optimization_barrier(jnp.mean(values_in * values_in, -1, keepdims=True)) + 1e-06)

def reference(tokens, owner_shard, dest_slot, w_qkv, w_out, norm_gain, norm_shift, query_gain, key_gain, out_gate):
    destination = (owner_shard[:, 0] * MRG_SEQ + dest_slot).astype(jnp.int32)
    merged_sums = jax.ops.segment_sum(tokens.astype(jnp.float32), destination, num_segments=MERGED)
    row_mean = lax.optimization_barrier(jnp.mean(merged_sums, -1, keepdims=True))
    centered = merged_sums - row_mean
    row_var = lax.optimization_barrier(jnp.mean(centered * centered, -1, keepdims=True))
    normed = (centered * lax.rsqrt(row_var + 1e-06) * norm_gain + norm_shift).astype(jnp.bfloat16)
    projected = jnp.dot(normed, w_qkv.reshape(D, 3 * HEADS * HDIM), preferred_element_type=jnp.float32)
    projected = projected.reshape(MERGED, 3, HEADS, HDIM)
    queries = (rms_scale(projected[:, 0]) * query_gain / math.sqrt(HDIM)).astype(jnp.bfloat16)
    keys_all = (rms_scale(projected[:, 1]) * key_gain).astype(jnp.bfloat16).astype(jnp.float32)
    values_all = projected[:, 2].astype(jnp.bfloat16).astype(jnp.float32)

    def attend_block(query_block):
        scores = jnp.einsum('qhd,khd->hqk', query_block.astype(jnp.float32), keys_all)
        row_peak = lax.optimization_barrier(jnp.max(scores, -1, keepdims=True))
        expo = jnp.exp(scores - row_peak)
        denominator = lax.optimization_barrier(jnp.sum(expo, -1))
        expweights = lax.optimization_barrier(expo.astype(jnp.bfloat16)).astype(jnp.float32)
        numerator = jnp.einsum('hqk,khd->qhd', expweights, values_all)
        return (numerator / jnp.transpose(denominator)[:, :, None]).astype(jnp.bfloat16)
    blocks = queries.reshape(MERGED // 256, 256, HEADS, HDIM)
    attended = lax.map(attend_block, blocks).reshape(MERGED, HEADS * HDIM)
    merged_out = (jnp.dot(attended, w_out, preferred_element_type=jnp.float32) * out_gate).astype(jnp.bfloat16)
    return jnp.take(merged_out, destination, axis=0)
```

```python
import functools
import math

import jax
import jax.numpy as jnp
from jax import lax
from jax.experimental import pallas as pl
from jax.experimental.pallas import tpu as pltpu
from jax.sharding import PartitionSpec as P

HDIM = 128
RATIO = 4
MESH = pl.DeviceIdType.MESH
ANY = pl.BlockSpec(memory_space=pl.ANY)


def rms_scale(values_in):
    return values_in * lax.rsqrt(jnp.mean(values_in * values_in, -1, keepdims=True) + 1e-06)


def plane_width(seq_count):
    return 2 if seq_count % 2 == 0 else 1


class Plane:
    def __init__(self, seq_count, head_count):
        self.wide = plane_width(seq_count)
        self.heads = head_count
        self.size = self.wide * head_count

    def me(self):
        return lax.rem(lax.axis_index("seq"), self.wide) * self.heads + lax.axis_index("head")

    def device(self, index):
        base = lax.axis_index("seq") // self.wide * self.wide
        return (base + index // self.heads, lax.rem(index, self.heads))


class Line:
    def __init__(self, seq_count, head_count):
        self.wide = plane_width(seq_count)
        self.size = seq_count // self.wide

    def me(self):
        return lax.axis_index("seq") // self.wide

    def device(self, index):
        return (index * self.wide + lax.rem(lax.axis_index("seq"), self.wide), lax.axis_index("head"))


def greet(devices):
    barrier = pltpu.get_barrier_semaphore()
    for device in devices:
        pl.semaphore_signal(barrier, inc=1, device_id=device, device_id_type=MESH)
    pl.semaphore_wait(barrier, len(devices))


def gather_kernel(wide, length, count, *refs):
    sources, targets = [ref.at[pl.ds(1, 2)] for ref in refs[:count]], refs[count : 2 * count]
    line_send, line_recv, side_send, side_recv, own_sem = refs[2 * count :]
    seq, head = lax.axis_index("seq"), lax.axis_index("head")
    z, y = seq // wide, lax.rem(seq, wide)
    beside = [z * wide + lax.rem(y + turn, wide) for turn in range(1, wide)]
    along = [lax.rem(z + step, length) for step in range(1, length)]
    greet([(z * wide + lax.rem(y + turn, wide), head) for turn in range(1, wide)]
          + [(other * wide + y, head) for other in along])
    copies, arriving = [], []

    def begin(*ends):
        copy = remote(*ends)
        copy.start()
        return copy

    for step, other in enumerate(along):
        for item in range(count):
            arriving.append(begin(
                sources[item], targets[item].at[seq], line_send.at[item, step],
                line_recv.at[item, step], (other * wide + y, head)))
    for turn, other in enumerate(beside):
        for item in range(count):
            copies.append(begin(
                sources[item], targets[item].at[seq], side_send.at[item, turn, 0],
                side_recv.at[item, turn, 0], (other, head)))
    for item in range(count):
        own = pltpu.make_async_copy(sources[item], targets[item].at[seq], own_sem.at[item])
        own.start()
        copies.append(own)
    for step in range(length - 1):
        come = lax.rem(z + length - 1 - step, length) * wide + y
        for item in range(count):
            arriving[step * count + item].wait_recv()
            for turn, other in enumerate(beside):
                copies.append(begin(
                    targets[item].at[come], targets[item].at[come],
                    side_send.at[item, turn, step + 1], side_recv.at[item, turn, step + 1],
                    (other, head)))
    for copy in arriving:
        copy.wait_send()
    for copy in copies:
        copy.wait()


def gather_seq(number, seq_count, arrays):
    wide = plane_width(seq_count)
    length, count = seq_count // wide, len(arrays)
    return pl.pallas_call(
        functools.partial(gather_kernel, wide, length, count),
        out_shape=[jax.ShapeDtypeStruct((seq_count, 2, *a.shape[1:]), a.dtype) for a in arrays],
        in_specs=[ANY] * count,
        out_specs=[ANY] * count,
        scratch_shapes=[
            pltpu.SemaphoreType.DMA((count, length)),
            pltpu.SemaphoreType.DMA((count, length)),
            pltpu.SemaphoreType.DMA((count, wide, length)),
            pltpu.SemaphoreType.DMA((count, wide, length)),
            pltpu.SemaphoreType.DMA((count,)),
        ],
        compiler_params=pltpu.CompilerParams(collective_id=number, has_side_effects=True),
        name="gather_" + str(number),
    )(*arrays)


LANES = 128
VMEM = pl.BlockSpec(memory_space=pltpu.VMEM)


def remote(source, target, send, recv, device):
    return pltpu.make_async_remote_copy(
        src_ref=source, dst_ref=target, send_sem=send, recv_sem=recv,
        device_id=device, device_id_type=MESH,
    )


def to_row(column):
    return jnp.transpose(jnp.broadcast_to(column, (column.shape[0], LANES)))[:8]


def to_column(row):
    return jnp.transpose(jnp.broadcast_to(row, (LANES, row.shape[1])))[:, :1]


class Grid:
    def __init__(self, seq_count, head_count):
        self.wide = plane_width(seq_count)
        self.heads = head_count
        self.cores = 2 if head_count % 2 == 0 else 1
        self.length = seq_count // self.wide
        self.size = self.wide * head_count
        self.dims = (self.wide, head_count // self.cores, self.cores)
        seq, head = lax.axis_index("seq"), lax.axis_index("head")
        self.z, self.y = seq // self.wide, lax.rem(seq, self.wide)
        self.x, self.c = head // self.cores, lax.rem(head, self.cores)
        self.me = self.place(self.y, self.x, self.c)
        turns = [
            (ky, kx, kc)
            for ky in range(self.dims[0]) for kx in range(self.dims[1]) for kc in range(self.dims[2])
        ]
        self.turns = sorted(turns[1:], key=lambda turn: (turn[0] + turn[1], turn))
        self.chips = [turn for turn in self.turns if turn[2] == 0]

    def place(self, y, x, c):
        return (y * self.dims[1] + x) * self.cores + c

    def shifted(self, turn, sign):
        at = (self.y, self.x, self.c)
        return [lax.rem(at[i] + (sign * turn[i] + self.dims[i]), self.dims[i]) for i in range(3)]

    def to(self, turn):
        y, x, c = self.shifted(turn, 1)
        return self.place(y, x, c), self.device(self.z, y, x, c), y

    def source(self, turn):
        return self.place(*self.shifted(turn, -1))

    def device(self, z, y, x, c):
        return (z * self.wide + y, x * self.cores + c)

    def along(self, z):
        return self.device(z, self.y, self.x, self.c)

    def sibling(self):
        return self.device(self.z, self.y, self.x, lax.rem(self.c + 1, 2))

    def greet(self):
        barrier = pltpu.get_barrier_semaphore()
        last = self.length - 1

        def hail(device):
            pl.semaphore_signal(barrier, inc=1, device_id=device, device_id_type=MESH)

        for turn in self.turns:
            hail(self.to(turn)[1])

        @pl.when(self.z > 0)
        def _():
            hail(self.along(self.z - 1))

        @pl.when(self.z < last)
        def _():
            hail(self.along(self.z + 1))

        inner = jnp.where((self.z > 0) & (self.z < last), 1, 0)
        pl.semaphore_wait(barrier, len(self.turns) + 1 + inner)


def steps(count, body, reverse=False):
    if count <= 8:
        for number in reversed(range(count)) if reverse else range(count):
            body(number)
    else:
        def one(number, carry):
            body(count - 1 - number if reverse else number)
            return carry
        lax.fori_loop(0, count, one, 0)


def front_kernel(
    seq_count, head_count, chunks, cached, tokens, owners, slots, gain, shift, normed, all_ids, seen,
    far, far_ids, hot, hot_far, part, passing, sums, raw, id_send, id_recv, far_id_send,
    far_id_recv, seen_send, seen_recv, own_sem, far_send, far_recv, pass_send, pass_recv,
    raw_send, raw_recv, twin_send, twin_recv,
):
    grid = Grid(seq_count, head_count)
    z, me, length = grid.z, grid.me, grid.length
    src_rows = tokens.shape[0]
    rows = sums.shape[1]
    merged_rows = rows // grid.wide
    width = chunks * LANES
    feature_width = width * grid.size
    low = z < (length + 1) // 2
    sign = jnp.where(low, 1, -1)
    home = jnp.where(low, z, length - 1 - z)
    inward = jnp.where(low, 1, 0)
    outward = 1 - inward
    at_end, near = home == 0, home == 1

    def slab(index, chunk):
        return pl.ds(pl.multiple_of(index * width + chunk * LANES, LANES), LANES)

    owner_row = jnp.transpose(
        jnp.broadcast_to(owners[...].astype(jnp.float32), (src_rows, LANES))
    )[:1].astype(jnp.int32)
    all_ids[me] = owner_row * merged_rows + slots[...]
    grid.greet()
    id_copies, seen_copies, owns = [], [], []
    for step, turn in enumerate(grid.turns):
        copy = remote(all_ids.at[me], all_ids.at[me], id_send.at[step], id_recv.at[step], grid.to(turn)[1])
        copy.start()
        id_copies.append(copy)
    for chunk in range(chunks):
        own = pltpu.make_async_copy(tokens.at[:, slab(me, chunk)], seen.at[chunk, me], own_sem.at[chunk])
        own.start()
        owns.append(own)
        copies = []
        for step, turn in enumerate(grid.turns):
            index, device, _ = grid.to(turn)
            copy = remote(tokens.at[:, slab(index, chunk)], seen.at[chunk, me],
                          seen_send.at[chunk, step], seen_recv.at[chunk, step], device)
            copy.start()
            copies.append(copy)
        seen_copies.append(copies)

    def far_block(chunk, index):
        return remote(seen.at[chunk, index], far.at[chunk, index], far_send.at[chunk],
                      far_recv.at[chunk], grid.along(z + sign))

    def far_whole(chunk):
        return remote(seen.at[chunk], far.at[chunk], far_send.at[chunk], far_recv.at[chunk],
                      grid.along(z + sign))

    far_names = remote(all_ids, far_ids, far_id_send, far_id_recv, grid.along(z + sign))
    for copy in id_copies:
        copy.wait_recv()

    @pl.when(at_end)
    def _():
        far_names.start()

    places = lax.broadcasted_iota(jnp.int32, (rows, 1), 0)

    def marks(names, dest):
        labels = jnp.concatenate([names[index] for index in range(grid.size)], axis=1)
        return (places + dest * rows == labels).astype(jnp.float32).astype(jnp.bfloat16)

    def summed(chunk, dest):
        chosen = hot[dest] if cached else marks(all_ids, dest)
        return jnp.dot(chosen, seen[chunk].reshape(grid.size * src_rows, LANES),
                       preferred_element_type=jnp.float32)

    def summed_far(chunk, dest):
        chosen = hot_far[dest] if cached else marks(far_ids, dest)
        return jnp.dot(chosen, far[chunk].reshape(grid.size * src_rows, LANES),
                       preferred_element_type=jnp.float32)

    if cached:
        for dest in range(length):
            hot[dest] = marks(all_ids, dest)

        @pl.when(near)
        def _():
            far_names.wait_recv()
            for dest in range(length):
                hot_far[dest] = marks(far_ids, dest)
    else:
        @pl.when(near)
        def _():
            far_names.wait_recv()

    @pl.when(at_end)
    def _():
        for chunk in range(chunks):
            owns[chunk].wait()
            far_block(chunk, me).start()
            for step, turn in enumerate(grid.turns):
                seen_copies[chunk][step].wait_recv()
                far_block(chunk, grid.source(turn)).start()
            part[chunk, z] = summed(chunk, z)

    def away_copy(chunk, dest):
        spot = dest + inward
        return remote(part.at[chunk, dest], passing.at[chunk, spot], pass_send.at[chunk, spot],
                      pass_recv.at[chunk, spot], grid.along(z + sign))

    def home_copy(chunk, dest):
        spot = dest + outward
        return remote(part.at[chunk, dest], passing.at[chunk, spot], pass_send.at[chunk, spot],
                      pass_recv.at[chunk, spot], grid.along(z - sign))

    def away(chunk):
        def one(back):
            far_off = back + 1

            @pl.when(far_off <= length - 1 - home)
            def _():
                dest = z + sign * far_off
                part[chunk, dest] = summed(chunk, dest)

                @pl.when(near)
                def _():
                    part[chunk, dest] += summed_far(chunk, dest)

                @pl.when(home >= 2)
                def _():
                    away_copy(chunk, dest).wait_recv()
                    part[chunk, dest] += passing[chunk, dest + inward]

                away_copy(chunk, dest).start()

        steps(length - 1, one, reverse=True)
        part[chunk, z] = summed(chunk, z)

        @pl.when(near)
        def _():
            part[chunk, z] += summed_far(chunk, z)

    def homeward(chunk):
        def one(back):
            far_off = back + 1

            @pl.when(far_off <= home)
            def _():
                dest = z - sign * far_off
                part[chunk, dest] = summed(chunk, dest)
                home_copy(chunk, dest).wait_recv()
                part[chunk, dest] += passing[chunk, dest + outward]
                home_copy(chunk, dest).start()

        steps((length + 1) // 2 - 1, one, reverse=True)

    def my_rows(y):
        return pl.ds(pl.multiple_of(y * merged_rows, merged_rows), merged_rows)

    raw_copies, twin_copies = [], []

    def finish(chunk):
        @pl.when(home >= 2)
        def _():
            away_copy(chunk, z).wait_recv()
            part[chunk, z] += passing[chunk, z + inward]

        home_copy(chunk, z).wait_recv()
        sums[chunk] = part[chunk, z] + passing[chunk, z + outward]
        copies, twins = [], []
        for step, turn in enumerate(grid.chips):
            _, device, y = grid.to(turn)
            copy = remote(sums.at[chunk, my_rows(y)], raw.at[me * chunks + chunk],
                          raw_send.at[chunk, step], raw_recv.at[chunk, step], device)
            copy.start()
            copies.append(copy)
        raw[me * chunks + chunk] = sums[chunk, my_rows(grid.y)]
        raw_copies.append(copies)
        twin_copies.append(twins)
        hand_over(chunk, me, len(grid.chips))

    def hand_over(chunk, index, step):
        if grid.cores == 1:
            return
        spot = raw.at[index * chunks + chunk]
        copy = remote(spot, spot, twin_send.at[chunk, step], twin_recv.at[chunk, step], grid.sibling())
        copy.start()
        twin_copies[chunk].append(copy)

    def pass_over(chunk):
        for step, turn in enumerate(grid.chips):
            raw_copies[chunk][step].wait_recv()
            hand_over(chunk, grid.source(turn), step)

    for chunk in range(chunks):
        @pl.when(jnp.logical_not(at_end))
        def _():
            owns[chunk].wait()
            for copy in seen_copies[chunk]:
                copy.wait_recv()

            @pl.when(near)
            def _():
                far_whole(chunk).wait_recv()

            away(chunk)

        if chunk > 0:
            finish(chunk - 1)
        if chunk > 1:
            pass_over(chunk - 2)

        @pl.when(jnp.logical_not(at_end))
        def _():
            homeward(chunk)

    finish(chunks - 1)
    for chunk in range(max(chunks - 2, 0), chunks):
        pass_over(chunk)
    for copies in twin_copies:
        for copy in copies:
            copy.wait_recv()
    blocks = grid.size * chunks
    acc = raw[0]
    for block in range(1, blocks):
        acc += raw[block]
    mean = jnp.sum(acc, -1, keepdims=True) * (1.0 / feature_width)
    acc = jnp.zeros_like(acc)
    for block in range(blocks):
        apart = raw[block] - mean
        acc += apart * apart
    scale = lax.rsqrt(jnp.sum(acc, -1, keepdims=True) * (1.0 / feature_width) + 1e-06)
    for block in range(blocks):
        spot = slice(block * LANES, (block + 1) * LANES)
        normed[:, spot] = ((raw[block] - mean) * scale * gain[:, spot] + shift[:, spot]).astype(jnp.bfloat16)

    for copy in id_copies:
        copy.wait_send()
    for chunk in range(chunks):
        for copy in seen_copies[chunk] + raw_copies[chunk] + twin_copies[chunk]:
            copy.wait_send()

    @pl.when(at_end)
    def _():
        far_names.wait_send()
        for chunk in range(chunks):
            far_whole(chunk).wait_send()

    @pl.when(jnp.logical_not(at_end))
    def _():
        for chunk in range(chunks):
            def sent(number):
                @pl.when(number + 1 <= length - 1 - home)
                def _():
                    away_copy(chunk, z + sign * (number + 1)).wait_send()

                @pl.when(number + 1 <= home)
                def _():
                    home_copy(chunk, z - sign * (number + 1)).wait_send()

            steps(length - 1, sent)


def front(number, tokens, owners, slots, gain, shift):
    seq_count, head_count = lax.axis_size("seq"), lax.axis_size("head")
    wide = plane_width(seq_count)
    length, size = seq_count // wide, wide * head_count
    src_rows, feature_width = tokens.shape
    chunks = feature_width // size // LANES
    merged_rows = src_rows * head_count // RATIO
    rows = wide * merged_rows
    labels = size * src_rows
    cached = length * rows * labels * 4 <= 8 * 2**20
    marks_shape = (length, rows, labels) if cached else (1, 16, LANES)
    dma, turns, chips = pltpu.SemaphoreType.DMA, size - 1, size // 2
    return pl.pallas_call(
        functools.partial(front_kernel, seq_count, head_count, chunks, cached),
        out_shape=[
            jax.ShapeDtypeStruct((merged_rows, feature_width), jnp.bfloat16),
            jax.ShapeDtypeStruct((size, 1, src_rows), jnp.int32),
        ],
        in_specs=[ANY] + [VMEM] * 4,
        out_specs=[VMEM] * 2,
        scratch_shapes=[
            pltpu.VMEM((chunks, size, src_rows, LANES), jnp.bfloat16),
            pltpu.VMEM((chunks, size, src_rows, LANES), jnp.bfloat16),
            pltpu.VMEM((size, 1, src_rows), jnp.int32),
            pltpu.VMEM(marks_shape, jnp.bfloat16),
            pltpu.VMEM(marks_shape, jnp.bfloat16),
            pltpu.VMEM((chunks, length, rows, LANES), jnp.float32),
            pltpu.VMEM((chunks, length + 1, rows, LANES), jnp.float32),
            pltpu.VMEM((chunks, rows, LANES), jnp.float32),
            pltpu.VMEM((size * chunks, merged_rows, LANES), jnp.float32),
            dma((turns,)),
            dma((turns,)),
            dma(()),
            dma(()),
            dma((chunks, turns)),
            dma((chunks, turns)),
            dma((chunks,)),
            dma((chunks,)),
            dma((chunks,)),
            dma((chunks, length + 1)),
            dma((chunks, length + 1)),
            dma((chunks, chips)),
            dma((chunks, chips)),
            dma((chunks, chips)),
            dma((chunks, chips)),
        ],
        compiler_params=pltpu.CompilerParams(
            collective_id=number, has_side_effects=True, vmem_limit_bytes=56 * 2**20
        ),
        name="front",
    )(tokens, owners, slots, gain, shift)


def project_kernel(normed, weights, gains, out):
    made = jnp.dot(normed[...], weights[0], preferred_element_type=jnp.float32)
    plain = pl.program_id(0) == 2
    for start in range(0, made.shape[1], HDIM):
        one = made[:, start:start + HDIM]
        scaled = rms_scale(one) * gains[0]
        out[0, :, start:start + HDIM] = jnp.where(plain, one, scaled).astype(jnp.bfloat16)


def project(normed, weights, gains):
    rows, depth = normed.shape
    width = weights.shape[2]
    return pl.pallas_call(
        project_kernel,
        grid=(3,),
        out_shape=jax.ShapeDtypeStruct((3, rows, width), jnp.bfloat16),
        in_specs=[
            pl.BlockSpec((rows, depth), lambda j: (0, 0)),
            pl.BlockSpec((1, depth, width), lambda j: (j, 0, 0)),
            pl.BlockSpec((1, 1, HDIM), lambda j: (j, 0, 0)),
        ],
        out_specs=pl.BlockSpec((1, rows, width), lambda j: (j, 0, 0)),
        compiler_params=pltpu.CompilerParams(vmem_limit_bytes=56 * 2**20),
        name="project",
    )(normed, weights, gains)


def attend_kernel(mine, pairs, w_out, partial):
    rows, width = mine.shape[1], mine.shape[2]
    heads = []
    for start in range(0, width, HDIM):
        spot = slice(start, start + HDIM)
        keys = pairs[:, 0, :, spot].reshape(-1, HDIM)
        values = pairs[:, 1, :, spot].reshape(-1, HDIM)
        scores = lax.dot_general(
            mine[0, :, spot], keys, (((1,), (1,)), ((), ())), preferred_element_type=jnp.float32
        )
        expo = jnp.exp(scores - jnp.max(scores, -1, keepdims=True))
        total = jnp.sum(expo, -1, keepdims=True)
        weighted = jnp.dot(expo.astype(jnp.bfloat16), values, preferred_element_type=jnp.float32)
        heads.append((weighted / total).astype(jnp.bfloat16))
    attended = jnp.concatenate(heads, axis=1)
    partial[...] = jnp.dot(
        attended, w_out[...], preferred_element_type=jnp.float32
    ).astype(jnp.bfloat16)


def tail_kernel(
    plane, line, chunks, mine, pairs, w_out, gate, ids, out, partial, pieces, merged, chooser,
    fetched, piece_send, piece_recv, up_send, up_recv, down_send, down_recv, back_send, back_recv,
):
    me, z, length = plane.me(), line.me(), line.size
    src_rows = out.shape[0]
    rows = merged.shape[2]
    merged_rows = rows // plane.wide
    width = chunks * LANES
    others = [lax.rem(me + step, plane.size) for step in range(1, plane.size)]
    devices = [plane.device(other) for other in others]
    above, below = lax.rem(z + 1, length), lax.rem(z + length - 1, length)
    along = [lax.rem(z + step, length) for step in range(1, length)]
    greet(devices + [line.device(other) for other in along])

    def slab(index, chunk):
        return pl.ds(pl.multiple_of(index * width + chunk * LANES, LANES), LANES)

    attend_kernel(mine, pairs, w_out, partial)
    started = []

    def go(copy):
        copy.start()
        started.append(copy)
        return copy

    piece_copies = [
        [
            go(remote(partial.at[:, slab(other, chunk)], pieces.at[chunk, me],
                      piece_send.at[chunk, step], piece_recv.at[chunk, step], devices[step]))
            for step, other in enumerate(others)
        ]
        for chunk in range(chunks)
    ]
    for chunk in range(chunks):
        pieces[chunk, me] = partial[:, slab(me, chunk)]
    places = lax.broadcasted_iota(jnp.int32, (1, length * rows), 1)
    for index in range(plane.size):
        chooser[index * src_rows:(index + 1) * src_rows] = (
            (to_column(ids[index]) == places).astype(jnp.float32).astype(jnp.bfloat16)
        )

    def upward(chunk, far):
        spot = merged.at[chunk, z - far]
        return remote(spot, spot, up_send.at[chunk, far], up_recv.at[chunk, far], line.device(above))

    def downward(chunk, far):
        spot = merged.at[chunk, z + far]
        return remote(spot, spot, down_send.at[chunk, far], down_recv.at[chunk, far],
                      line.device(below))

    def came_up(chunk, far):
        spot = merged.at[chunk, z - far]
        return remote(spot, spot, up_send.at[chunk, far - 1], up_recv.at[chunk, far - 1],
                      line.device(above))

    def came_down(chunk, far):
        spot = merged.at[chunk, z + far]
        return remote(spot, spot, down_send.at[chunk, far - 1], down_recv.at[chunk, far - 1],
                      line.device(below))

    def pass_on(chunk, far):
        if far < length - 1:
            @pl.when((z >= far) & (z < length - 1))
            def _():
                upward(chunk, far).start()

            @pl.when((z + far < length) & (z > 0))
            def _():
                downward(chunk, far).start()

    for turn in range(chunks + length - 1):
        for far in range(length):
            chunk = turn - far
            if not 0 <= chunk < chunks:
                continue
            if far == 0:
                for copy in piece_copies[chunk]:
                    copy.wait_recv()
                for y in range(plane.wide):
                    total = sum(
                        [
                            pieces[chunk, y * plane.heads + head].astype(jnp.float32)
                            for head in range(plane.heads)
                        ]
                    )
                    merged[chunk, z, y * merged_rows:(y + 1) * merged_rows] = (
                        total * gate[:, slab(me, chunk)]
                    ).astype(jnp.bfloat16)
            else:
                @pl.when(z >= far)
                def _():
                    came_up(chunk, far).wait_recv()

                @pl.when(z + far < length)
                def _():
                    came_down(chunk, far).wait_recv()
            pass_on(chunk, far)
            if far == length - 1:
                fetched[chunk] = (
                    jnp.dot(
                        chooser[...],
                        merged[chunk].reshape(length * rows, LANES),
                        preferred_element_type=jnp.float32,
                    )
                    .astype(jnp.bfloat16)
                    .reshape(plane.size, src_rows, LANES)
                )
                for step, other in enumerate(others):
                    go(remote(fetched.at[chunk, other], out.at[:, slab(me, chunk)],
                              back_send.at[chunk, step], back_recv.at[chunk, step], devices[step]))
                out[:, slab(me, chunk)] = fetched[chunk, me]
    for chunk in range(chunks):
        for far in range(length - 1):
            @pl.when((z >= far) & (z < length - 1))
            def _():
                upward(chunk, far).wait_send()

            @pl.when((z + far < length) & (z > 0))
            def _():
                downward(chunk, far).wait_send()
    backs = started[len(others) * chunks:]
    for copy in backs:
        copy.wait_recv()
    for copy in started:
        copy.wait_send()


def tail(number, plane, line, made, pairs, w_out, gate, ids):
    src_rows, feature_width = ids.shape[2], w_out.shape[1]
    merged_rows = made.shape[1]
    width = feature_width // plane.size
    chunks = width // LANES
    rows = plane.wide * merged_rows
    dma = pltpu.SemaphoreType.DMA
    others = plane.size - 1
    return pl.pallas_call(
        functools.partial(tail_kernel, plane, line, chunks),
        out_shape=jax.ShapeDtypeStruct((src_rows, feature_width), jnp.bfloat16),
        in_specs=[VMEM] * 5,
        out_specs=VMEM,
        scratch_shapes=[
            pltpu.VMEM((merged_rows, feature_width), jnp.bfloat16),
            pltpu.VMEM((chunks, plane.size, merged_rows, LANES), jnp.bfloat16),
            pltpu.VMEM((chunks, line.size, rows, LANES), jnp.bfloat16),
            pltpu.VMEM((plane.size * src_rows, line.size * rows), jnp.bfloat16),
            pltpu.VMEM((chunks, plane.size, src_rows, LANES), jnp.bfloat16),
            dma((chunks, others)),
            dma((chunks, others)),
            dma((chunks, line.size)),
            dma((chunks, line.size)),
            dma((chunks, line.size)),
            dma((chunks, line.size)),
            dma((chunks, others)),
            dma((chunks, others)),
        ],
        compiler_params=pltpu.CompilerParams(
            collective_id=number, has_side_effects=True, vmem_limit_bytes=56 * 2**20
        ),
        name="tail",
    )(made, pairs, w_out, gate, ids)


def on_device(
    tokens,
    owner_shard,
    dest_slot,
    w_qkv,
    w_out,
    norm_gain,
    norm_shift,
    query_gain,
    key_gain,
    out_gate,
):
    seq_count = lax.axis_size("seq")
    head_count = lax.axis_size("head")
    plane, line = Plane(seq_count, head_count), Line(seq_count, head_count)
    normed, seen_ids = front(0, tokens, owner_shard, dest_slot[None], norm_gain[None], norm_shift[None])
    gains = jnp.stack([query_gain / math.sqrt(HDIM), key_gain, jnp.ones_like(key_gain)])
    made = project(normed, jnp.transpose(w_qkv, (1, 0, 2)), gains[:, None])
    [pairs] = gather_seq(4, seq_count, [made])
    return tail(5, plane, line, made, pairs, w_out, out_gate[None], seen_ids)


def solution(mesh):
    placed = (
        P(("seq", "head"), None),
        P(("seq", "head"), None),
        P(("seq", "head")),
        P(None, None, "head"),
        P("head", None),
        P(),
        P(),
        P(),
        P(),
        P(),
    )
    return jax.shard_map(
        on_device, mesh=mesh, in_specs=placed, out_specs=P(("seq", "head"), None), check_vma=False
    )
```

```python
import functools
import math

import jax
import jax.numpy as jnp
from jax import lax
from jax.experimental import pallas as pl
from jax.experimental.pallas import tpu as pltpu
from jax.sharding import PartitionSpec as P

HDIM = 128
RATIO = 4
MESH = pl.DeviceIdType.MESH
ANY = pl.BlockSpec(memory_space=pl.ANY)


def rms_scale(values_in):
    return values_in * lax.rsqrt(jnp.mean(values_in * values_in, -1, keepdims=True) + 1e-06)


def plane_width(seq_count):
    return 2 if seq_count % 2 == 0 else 1


LANES = 128
VMEM = pl.BlockSpec(memory_space=pltpu.VMEM)


def remote(source, target, send, recv, device):
    return pltpu.make_async_remote_copy(
        src_ref=source, dst_ref=target, send_sem=send, recv_sem=recv,
        device_id=device, device_id_type=MESH,
    )


def to_column(row):
    return jnp.transpose(jnp.broadcast_to(row, (LANES, row.shape[1])))[:, :1]


class Grid:
    def __init__(self, seq_count, head_count):
        self.wide = plane_width(seq_count)
        self.heads = head_count
        self.cores = 2 if head_count % 2 == 0 else 1
        self.length = seq_count // self.wide
        self.size = self.wide * head_count
        self.dims = (self.wide, head_count // self.cores, self.cores)
        seq, head = lax.axis_index("seq"), lax.axis_index("head")
        self.z, self.y = seq // self.wide, lax.rem(seq, self.wide)
        self.x, self.c = head // self.cores, lax.rem(head, self.cores)
        self.me = self.place(self.y, self.x, self.c)
        turns = [
            (ky, kx, kc)
            for ky in range(self.dims[0]) for kx in range(self.dims[1]) for kc in range(self.dims[2])
        ]
        self.turns = sorted(turns[1:], key=lambda turn: (turn[0] + turn[1], turn))
        self.chips = [turn for turn in self.turns if turn[2] == 0]

    def place(self, y, x, c):
        return (y * self.dims[1] + x) * self.cores + c

    def shifted(self, turn, sign):
        at = (self.y, self.x, self.c)
        return [lax.rem(at[i] + (sign * turn[i] + self.dims[i]), self.dims[i]) for i in range(3)]

    def to(self, turn):
        y, x, c = self.shifted(turn, 1)
        return self.place(y, x, c), self.device(self.z, y, x, c), y

    def source(self, turn):
        return self.place(*self.shifted(turn, -1))

    def device(self, z, y, x, c):
        return (z * self.wide + y, x * self.cores + c)

    def along(self, z):
        return self.device(z, self.y, self.x, self.c)

    def sibling(self):
        return self.device(self.z, self.y, self.x, lax.rem(self.c + 1, 2))

    def greet(self):
        barrier = pltpu.get_barrier_semaphore()
        last = self.length - 1

        def hail(device):
            pl.semaphore_signal(barrier, inc=1, device_id=device, device_id_type=MESH)

        for turn in self.turns:
            hail(self.to(turn)[1])

        @pl.when(self.z > 0)
        def _():
            hail(self.along(self.z - 1))

        @pl.when(self.z < last)
        def _():
            hail(self.along(self.z + 1))

        inner = jnp.where((self.z > 0) & (self.z < last), 1, 0)
        pl.semaphore_wait(barrier, len(self.turns) + 1 + inner)


def steps(count, body, reverse=False):
    if count <= 8:
        for number in reversed(range(count)) if reverse else range(count):
            body(number)
    else:
        def one(number, carry):
            body(count - 1 - number if reverse else number)
            return carry
        lax.fori_loop(0, count, one, 0)


def front_kernel(
    seq_count, head_count, chunks, cached, tokens, owners, slots, gain, shift, normed, all_ids, seen,
    far, far_ids, hot, hot_far, part, passing, sums, raw, id_send, id_recv, far_id_send,
    far_id_recv, seen_send, seen_recv, own_sem, far_send, far_recv, pass_send, pass_recv,
    raw_send, raw_recv, twin_send, twin_recv,
):
    grid = Grid(seq_count, head_count)
    z, me, length = grid.z, grid.me, grid.length
    src_rows = tokens.shape[0]
    rows = sums.shape[1]
    merged_rows = rows // grid.wide
    width = chunks * LANES
    feature_width = width * grid.size
    low = z < (length + 1) // 2
    sign = jnp.where(low, 1, -1)
    home = jnp.where(low, z, length - 1 - z)
    inward = jnp.where(low, 1, 0)
    outward = 1 - inward
    at_end, near = home == 0, home == 1

    def slab(index, chunk):
        return pl.ds(pl.multiple_of(index * width + chunk * LANES, LANES), LANES)

    owner_row = jnp.transpose(
        jnp.broadcast_to(owners[...].astype(jnp.float32), (src_rows, LANES))
    )[:1].astype(jnp.int32)
    all_ids[me] = owner_row * merged_rows + slots[...]
    grid.greet()
    id_copies, seen_copies, owns = [], [], []
    for step, turn in enumerate(grid.turns):
        copy = remote(all_ids.at[me], all_ids.at[me], id_send.at[step], id_recv.at[step], grid.to(turn)[1])
        copy.start()
        id_copies.append(copy)
    for chunk in range(chunks):
        own = pltpu.make_async_copy(tokens.at[:, slab(me, chunk)], seen.at[chunk, me], own_sem.at[chunk])
        own.start()
        owns.append(own)
        copies = []
        for step, turn in enumerate(grid.turns):
            index, device, _ = grid.to(turn)
            copy = remote(tokens.at[:, slab(index, chunk)], seen.at[chunk, me],
                          seen_send.at[chunk, step], seen_recv.at[chunk, step], device)
            copy.start()
            copies.append(copy)
        seen_copies.append(copies)

    def far_block(chunk, index):
        return remote(seen.at[chunk, index], far.at[chunk, index], far_send.at[chunk],
                      far_recv.at[chunk], grid.along(z + sign))

    def far_whole(chunk):
        return remote(seen.at[chunk], far.at[chunk], far_send.at[chunk], far_recv.at[chunk],
                      grid.along(z + sign))

    far_names = remote(all_ids, far_ids, far_id_send, far_id_recv, grid.along(z + sign))
    for copy in id_copies:
        copy.wait_recv()

    @pl.when(at_end)
    def _():
        far_names.start()

    places = lax.broadcasted_iota(jnp.int32, (rows, 1), 0)

    def marks(names, dest):
        labels = jnp.concatenate([names[index] for index in range(grid.size)], axis=1)
        return (places + dest * rows == labels).astype(jnp.float32).astype(jnp.bfloat16)

    def summed(chunk, dest):
        chosen = hot[dest] if cached else marks(all_ids, dest)
        return jnp.dot(chosen, seen[chunk].reshape(grid.size * src_rows, LANES),
                       preferred_element_type=jnp.float32)

    def summed_far(chunk, dest):
        chosen = hot_far[dest] if cached else marks(far_ids, dest)
        return jnp.dot(chosen, far[chunk].reshape(grid.size * src_rows, LANES),
                       preferred_element_type=jnp.float32)

    if cached:
        for dest in range(length):
            hot[dest] = marks(all_ids, dest)

        @pl.when(near)
        def _():
            far_names.wait_recv()
            for dest in range(length):
                hot_far[dest] = marks(far_ids, dest)
    else:
        @pl.when(near)
        def _():
            far_names.wait_recv()

    @pl.when(at_end)
    def _():
        for chunk in range(chunks):
            owns[chunk].wait()
            far_block(chunk, me).start()
            for step, turn in enumerate(grid.turns):
                seen_copies[chunk][step].wait_recv()
                far_block(chunk, grid.source(turn)).start()
            part[chunk, z] = summed(chunk, z)

    def away_copy(chunk, dest):
        spot = dest + inward
        return remote(part.at[chunk, dest], passing.at[chunk, spot], pass_send.at[chunk, spot],
                      pass_recv.at[chunk, spot], grid.along(z + sign))

    def home_copy(chunk, dest):
        spot = dest + outward
        return remote(part.at[chunk, dest], passing.at[chunk, spot], pass_send.at[chunk, spot],
                      pass_recv.at[chunk, spot], grid.along(z - sign))

    def away(chunk):
        def one(back):
            far_off = back + 1

            @pl.when(far_off <= length - 1 - home)
            def _():
                dest = z + sign * far_off
                part[chunk, dest] = summed(chunk, dest)

                @pl.when(near)
                def _():
                    part[chunk, dest] += summed_far(chunk, dest)

                @pl.when(home >= 2)
                def _():
                    away_copy(chunk, dest).wait_recv()
                    part[chunk, dest] += passing[chunk, dest + inward]

                away_copy(chunk, dest).start()

        steps(length - 1, one, reverse=True)
        part[chunk, z] = summed(chunk, z)

        @pl.when(near)
        def _():
            part[chunk, z] += summed_far(chunk, z)

    def homeward(chunk):
        def one(back):
            far_off = back + 1

            @pl.when(far_off <= home)
            def _():
                dest = z - sign * far_off
                part[chunk, dest] = summed(chunk, dest)
                home_copy(chunk, dest).wait_recv()
                part[chunk, dest] += passing[chunk, dest + outward]
                home_copy(chunk, dest).start()

        steps((length + 1) // 2 - 1, one, reverse=True)

    def my_rows(y):
        return pl.ds(pl.multiple_of(y * merged_rows, merged_rows), merged_rows)

    raw_copies, twin_copies = [], []

    def finish(chunk):
        @pl.when(home >= 2)
        def _():
            away_copy(chunk, z).wait_recv()
            part[chunk, z] += passing[chunk, z + inward]

        home_copy(chunk, z).wait_recv()
        sums[chunk] = part[chunk, z] + passing[chunk, z + outward]
        copies, twins = [], []
        for step, turn in enumerate(grid.chips):
            _, device, y = grid.to(turn)
            copy = remote(sums.at[chunk, my_rows(y)], raw.at[me * chunks + chunk],
                          raw_send.at[chunk, step], raw_recv.at[chunk, step], device)
            copy.start()
            copies.append(copy)
        raw[me * chunks + chunk] = sums[chunk, my_rows(grid.y)]
        raw_copies.append(copies)
        twin_copies.append(twins)
        hand_over(chunk, me, len(grid.chips))

    def hand_over(chunk, index, step):
        if grid.cores == 1:
            return
        spot = raw.at[index * chunks + chunk]
        copy = remote(spot, spot, twin_send.at[chunk, step], twin_recv.at[chunk, step], grid.sibling())
        copy.start()
        twin_copies[chunk].append(copy)

    def pass_over(chunk):
        for step, turn in enumerate(grid.chips):
            raw_copies[chunk][step].wait_recv()
            hand_over(chunk, grid.source(turn), step)

    for chunk in range(chunks):
        @pl.when(jnp.logical_not(at_end))
        def _():
            owns[chunk].wait()
            for copy in seen_copies[chunk]:
                copy.wait_recv()

            @pl.when(near)
            def _():
                far_whole(chunk).wait_recv()

            away(chunk)

        if chunk > 0:
            finish(chunk - 1)
        if chunk > 1:
            pass_over(chunk - 2)

        @pl.when(jnp.logical_not(at_end))
        def _():
            homeward(chunk)

    finish(chunks - 1)
    for chunk in range(max(chunks - 2, 0), chunks):
        pass_over(chunk)
    for copies in twin_copies:
        for copy in copies:
            copy.wait_recv()
    blocks = grid.size * chunks
    acc = raw[0]
    for block in range(1, blocks):
        acc += raw[block]
    mean = jnp.sum(acc, -1, keepdims=True) * (1.0 / feature_width)
    acc = jnp.zeros_like(acc)
    for block in range(blocks):
        apart = raw[block] - mean
        acc += apart * apart
    scale = lax.rsqrt(jnp.sum(acc, -1, keepdims=True) * (1.0 / feature_width) + 1e-06)
    for block in range(blocks):
        spot = slice(block * LANES, (block + 1) * LANES)
        normed[:, spot] = ((raw[block] - mean) * scale * gain[:, spot] + shift[:, spot]).astype(jnp.bfloat16)

    for copy in id_copies:
        copy.wait_send()
    for chunk in range(chunks):
        for copy in seen_copies[chunk] + raw_copies[chunk] + twin_copies[chunk]:
            copy.wait_send()

    @pl.when(at_end)
    def _():
        far_names.wait_send()
        for chunk in range(chunks):
            far_whole(chunk).wait_send()

    @pl.when(jnp.logical_not(at_end))
    def _():
        for chunk in range(chunks):
            def sent(number):
                @pl.when(number + 1 <= length - 1 - home)
                def _():
                    away_copy(chunk, z + sign * (number + 1)).wait_send()

                @pl.when(number + 1 <= home)
                def _():
                    home_copy(chunk, z - sign * (number + 1)).wait_send()

            steps(length - 1, sent)


def front(number, tokens, owners, slots, gain, shift):
    seq_count, head_count = lax.axis_size("seq"), lax.axis_size("head")
    wide = plane_width(seq_count)
    length, size = seq_count // wide, wide * head_count
    src_rows, feature_width = tokens.shape
    chunks = feature_width // size // LANES
    merged_rows = src_rows * head_count // RATIO
    rows = wide * merged_rows
    labels = size * src_rows
    cached = length * rows * labels * 4 <= 8 * 2**20
    marks_shape = (length, rows, labels) if cached else (1, 16, LANES)
    dma, turns, chips = pltpu.SemaphoreType.DMA, size - 1, size // 2
    return pl.pallas_call(
        functools.partial(front_kernel, seq_count, head_count, chunks, cached),
        out_shape=[
            jax.ShapeDtypeStruct((merged_rows, feature_width), jnp.bfloat16),
            jax.ShapeDtypeStruct((size, 1, src_rows), jnp.int32),
        ],
        in_specs=[ANY] + [VMEM] * 4,
        out_specs=[VMEM] * 2,
        scratch_shapes=[
            pltpu.VMEM((chunks, size, src_rows, LANES), jnp.bfloat16),
            pltpu.VMEM((chunks, size, src_rows, LANES), jnp.bfloat16),
            pltpu.VMEM((size, 1, src_rows), jnp.int32),
            pltpu.VMEM(marks_shape, jnp.bfloat16),
            pltpu.VMEM(marks_shape, jnp.bfloat16),
            pltpu.VMEM((chunks, length, rows, LANES), jnp.float32),
            pltpu.VMEM((chunks, length + 1, rows, LANES), jnp.float32),
            pltpu.VMEM((chunks, rows, LANES), jnp.float32),
            pltpu.VMEM((size * chunks, merged_rows, LANES), jnp.float32),
            dma((turns,)),
            dma((turns,)),
            dma(()),
            dma(()),
            dma((chunks, turns)),
            dma((chunks, turns)),
            dma((chunks,)),
            dma((chunks,)),
            dma((chunks,)),
            dma((chunks, length + 1)),
            dma((chunks, length + 1)),
            dma((chunks, chips)),
            dma((chunks, chips)),
            dma((chunks, chips)),
            dma((chunks, chips)),
        ],
        compiler_params=pltpu.CompilerParams(
            collective_id=number, has_side_effects=True, vmem_limit_bytes=56 * 2**20
        ),
        name="front",
    )(tokens, owners, slots, gain, shift)


def rest_kernel(
    seq_count, head_count, chunks, heads, normed, w_qkv, w_out, query_gain, key_gain, gate, ids, out,
    w_pair, w_query, w_last, pairs, queries, chooser, theirs, came, mine, leaving, pieces, merged, fetched,
    load_sem, ring_send, ring_recv, twin_send, twin_recv, piece_send, piece_recv, up_send, up_recv,
    down_send, down_recv, back_send, back_recv,
):
    grid = Grid(seq_count, head_count)
    z, me, length = grid.z, grid.me, grid.length
    src_rows = out.shape[0]
    merged_rows = normed.shape[0]
    rows = merged.shape[2]
    width = chunks * LANES
    half = seq_count // 2
    spot_in_ring = jnp.where(grid.y == 0, z, seq_count - 1 - z)

    def ring_device(position):
        position = lax.rem(position + seq_count, seq_count)
        low = position < length
        return grid.device(jnp.where(low, position, seq_count - 1 - position),
                           jnp.where(low, 0, 1), grid.x, grid.c)

    def slab(index, chunk):
        return pl.ds(pl.multiple_of(index * width + chunk * LANES, LANES), LANES)

    def cut(head):
        return pl.ds(head * HDIM, HDIM)

    loads = []
    for head in range(heads):
        for kind in range(2):
            loads.append(pltpu.make_async_copy(
                w_qkv.at[kind + 1, :, cut(head)], w_pair.at[head, :, cut(kind)], load_sem.at[head, kind]))
    load_query = pltpu.make_async_copy(w_qkv.at[0], w_query, load_sem.at[heads, 0])
    load_last = pltpu.make_async_copy(w_out, w_last, load_sem.at[heads, 1])
    for load in loads + [load_query, load_last]:
        load.start()
    grid.greet()

    def ring_copy(way, kind, head, step):
        sign = 1 - 2 * way
        origin = lax.rem(spot_in_ring - sign * (step - 1) + 2 * seq_count, seq_count)
        block = pairs.at[head, origin, kind]
        return remote(block, block, ring_send.at[way, kind, head, step - 1],
                      ring_recv.at[way, kind, head, step - 1], ring_device(spot_in_ring + sign))

    def reach(way, kind):
        return half if way == kind else half - 1

    lines = [(way, kind) for kind in range(2) for way in range(2)]
    for head in range(heads):
        loads[2 * head].wait()
        loads[2 * head + 1].wait()
        made = jnp.dot(normed[...], w_pair[head], preferred_element_type=jnp.float32)
        pairs[head, spot_in_ring, 0] = (rms_scale(made[:, :HDIM]) * key_gain[...]).astype(jnp.bfloat16)
        pairs[head, spot_in_ring, 1] = made[:, HDIM:].astype(jnp.bfloat16)
        for way, kind in lines:
            ring_copy(way, kind, head, 1).start()
    load_query.wait()
    made = jnp.dot(normed[...], w_query[...], preferred_element_type=jnp.float32)
    for head in range(heads):
        one = made[:, head * HDIM:(head + 1) * HDIM]
        queries[head] = (rms_scale(one) * (query_gain[...] / math.sqrt(HDIM))).astype(jnp.bfloat16)
    places = lax.broadcasted_iota(jnp.int32, (1, length * rows), 1)
    for index in range(grid.size):
        chooser[index * src_rows:(index + 1) * src_rows] = (
            (to_column(ids[index]) == places).astype(jnp.float32).astype(jnp.bfloat16)
        )

    def pass_round(back):
        step = back + 1
        for head in range(heads):
            for way, kind in lines:
                ring_copy(way, kind, head, step).wait_recv()

                if reach(way, kind) == half:
                    ring_copy(way, kind, head, step + 1).start()
                else:
                    @pl.when(step < half - 1)
                    def _():
                        ring_copy(way, kind, head, step + 1).start()

    steps(half - 1, pass_round)
    load_last.wait()
    attended = []
    for head in range(heads):
        for kind in range(2):
            ring_copy(kind, kind, head, half).wait_recv()
        keys = pairs[head, :, 0].reshape(-1, HDIM)
        values = pairs[head, :, 1].reshape(-1, HDIM)
        scores = lax.dot_general(
            queries[head], keys, (((1,), (1,)), ((), ())), preferred_element_type=jnp.float32
        )
        expo = jnp.exp(scores - jnp.max(scores, -1, keepdims=True))
        total = jnp.sum(expo, -1, keepdims=True)
        weighted = jnp.dot(expo.astype(jnp.bfloat16), values, preferred_element_type=jnp.float32)
        attended.append((weighted / total).astype(jnp.bfloat16))
    attended = jnp.concatenate(attended, axis=1)

    spots = [(0, 0, 0)] + grid.chips
    twin_copies = []

    def product(turn, flip):
        y, x, c = grid.shifted(turn, 1)
        if flip:
            c = lax.rem(c + 1, grid.cores)
        start = pl.multiple_of(grid.place(y, x, c) * width, LANES)
        return jnp.dot(attended, w_last[:, pl.ds(start, width)], preferred_element_type=jnp.float32)

    for number, turn in enumerate(spots):
        theirs[number] = product(turn, True)
        copy = remote(theirs.at[number], came.at[number], twin_send.at[number], twin_recv.at[number],
                      grid.sibling())
        copy.start()
        twin_copies.append(copy)
    for number, turn in enumerate(spots):
        mine[number] = product(turn, False)
    for number in range(len(spots)):
        twin_copies[number].wait_recv()
        mine[number] += came[number]
    started, piece_copies = [], []

    def go(copy):
        copy.start()
        started.append(copy)
        return copy

    for chunk in range(chunks):
        copies = []
        for step, turn in enumerate(grid.chips):
            leaving[chunk, step] = mine[step + 1, :, chunk * LANES:(chunk + 1) * LANES].astype(jnp.bfloat16)
            copies.append(go(remote(
                leaving.at[chunk, step], pieces.at[chunk, step], piece_send.at[chunk, step],
                piece_recv.at[chunk, step], grid.to(turn)[1])))
        piece_copies.append(copies)

    def collect(chunk):
        for copy in piece_copies[chunk]:
            copy.wait_recv()
        for ky in range(grid.wide):
            total = mine[0, :, chunk * LANES:(chunk + 1) * LANES] if ky == 0 else None
            for step, turn in enumerate(grid.chips):
                if turn[0] == ky:
                    piece = pieces[chunk, step].astype(jnp.float32)
                    total = piece if total is None else total + piece
            y = lax.rem(grid.y - ky + grid.wide, grid.wide)
            merged[chunk, z, pl.ds(pl.multiple_of(y * merged_rows, merged_rows), merged_rows)] = (
                total * gate[:, slab(me, chunk)]
            ).astype(jnp.bfloat16)

    def upward(chunk, far):
        spot = merged.at[chunk, z - far]
        return remote(spot, spot, up_send.at[chunk, far], up_recv.at[chunk, far], grid.along(z + 1))

    def downward(chunk, far):
        spot = merged.at[chunk, z + far]
        return remote(spot, spot, down_send.at[chunk, far], down_recv.at[chunk, far], grid.along(z - 1))

    def came_up(chunk, far):
        spot = merged.at[chunk, z - far]
        return remote(spot, spot, up_send.at[chunk, far - 1], up_recv.at[chunk, far - 1], grid.along(z + 1))

    def came_down(chunk, far):
        spot = merged.at[chunk, z + far]
        return remote(spot, spot, down_send.at[chunk, far - 1], down_recv.at[chunk, far - 1],
                      grid.along(z - 1))

    def pass_on(chunk, far):
        if far < length - 1:
            @pl.when((z >= far) & (z < length - 1))
            def _():
                upward(chunk, far).start()

            @pl.when((z + far < length) & (z > 0))
            def _():
                downward(chunk, far).start()

    back_copies = []
    for round_number in range(chunks + length - 1):
        for far in range(length):
            chunk = round_number - far
            if not 0 <= chunk < chunks:
                continue
            if far == 0:
                collect(chunk)
            else:
                @pl.when(z >= far)
                def _():
                    came_up(chunk, far).wait_recv()

                @pl.when(z + far < length)
                def _():
                    came_down(chunk, far).wait_recv()
            pass_on(chunk, far)
            if far == length - 1:
                fetched[chunk] = (
                    jnp.dot(
                        chooser[...],
                        merged[chunk].reshape(length * rows, LANES),
                        preferred_element_type=jnp.float32,
                    )
                    .astype(jnp.bfloat16)
                    .reshape(grid.size, src_rows, LANES)
                )
                for step, turn in enumerate(grid.turns):
                    index, device, _ = grid.to(turn)
                    back_copies.append(go(remote(
                        fetched.at[chunk, index], out.at[:, slab(me, chunk)], back_send.at[chunk, step],
                        back_recv.at[chunk, step], device)))
                out[:, slab(me, chunk)] = fetched[chunk, me]
    for head in range(heads):
        for way, kind in lines:
            def sent(back):
                ring_copy(way, kind, head, back + 1).wait_send()

            steps(reach(way, kind), sent)
    for copy in twin_copies:
        copy.wait_send()
    for chunk in range(chunks):
        for far in range(length - 1):
            @pl.when((z >= far) & (z < length - 1))
            def _():
                upward(chunk, far).wait_send()

            @pl.when((z + far < length) & (z > 0))
            def _():
                downward(chunk, far).wait_send()
    for copy in back_copies:
        copy.wait_recv()
    for copy in started:
        copy.wait_send()


def rest(number, normed, w_qkv, w_out, query_gain, key_gain, gate, ids):
    seq_count, head_count = lax.axis_size("seq"), lax.axis_size("head")
    wide = plane_width(seq_count)
    length, size = seq_count // wide, wide * head_count
    src_rows = ids.shape[2]
    merged_rows, feature_width = normed.shape
    inner = w_qkv.shape[2]
    heads = inner // HDIM
    width = feature_width // size
    chunks = width // LANES
    rows = wide * merged_rows
    spots = size // 2
    dma, half, others = pltpu.SemaphoreType.DMA, seq_count // 2, size - 1
    return pl.pallas_call(
        functools.partial(rest_kernel, seq_count, head_count, chunks, heads),
        out_shape=jax.ShapeDtypeStruct((src_rows, feature_width), jnp.bfloat16),
        in_specs=[VMEM, ANY, ANY] + [VMEM] * 4,
        out_specs=VMEM,
        scratch_shapes=[
            pltpu.VMEM((heads, feature_width, 2 * HDIM), jnp.bfloat16),
            pltpu.VMEM((feature_width, inner), jnp.bfloat16),
            pltpu.VMEM((inner, feature_width), jnp.bfloat16),
            pltpu.VMEM((heads, seq_count, 2, merged_rows, HDIM), jnp.bfloat16),
            pltpu.VMEM((heads, merged_rows, HDIM), jnp.bfloat16),
            pltpu.VMEM((size * src_rows, length * rows), jnp.bfloat16),
            pltpu.VMEM((spots, merged_rows, width), jnp.float32),
            pltpu.VMEM((spots, merged_rows, width), jnp.float32),
            pltpu.VMEM((spots, merged_rows, width), jnp.float32),
            pltpu.VMEM((chunks, spots, merged_rows, LANES), jnp.bfloat16),
            pltpu.VMEM((chunks, spots, merged_rows, LANES), jnp.bfloat16),
            pltpu.VMEM((chunks, length, rows, LANES), jnp.bfloat16),
            pltpu.VMEM((chunks, size, src_rows, LANES), jnp.bfloat16),
            dma((heads + 1, 2)),
            dma((2, 2, heads, half)),
            dma((2, 2, heads, half)),
            dma((spots,)),
            dma((spots,)),
            dma((chunks, spots)),
            dma((chunks, spots)),
            dma((chunks, length)),
            dma((chunks, length)),
            dma((chunks, length)),
            dma((chunks, length)),
            dma((chunks, others)),
            dma((chunks, others)),
        ],
        compiler_params=pltpu.CompilerParams(
            collective_id=number, has_side_effects=True, vmem_limit_bytes=60 * 2**20
        ),
        name="rest",
    )(normed, w_qkv, w_out, query_gain, key_gain, gate, ids)


def on_device(
    tokens,
    owner_shard,
    dest_slot,
    w_qkv,
    w_out,
    norm_gain,
    norm_shift,
    query_gain,
    key_gain,
    out_gate,
):
    normed, ids = front(0, tokens, owner_shard, dest_slot[None], norm_gain[None], norm_shift[None])
    return rest(1, normed, jnp.transpose(w_qkv, (1, 0, 2)), w_out, query_gain[None], key_gain[None],
                out_gate[None], ids)


def solution(mesh):
    placed = (
        P(("seq", "head"), None),
        P(("seq", "head"), None),
        P(("seq", "head")),
        P(None, None, "head"),
        P("head", None),
        P(),
        P(),
        P(),
        P(),
        P(),
    )
    return jax.shard_map(
        on_device, mesh=mesh, in_specs=placed, out_specs=P(("seq", "head"), None), check_vma=False
    )
```

```python
import functools
import math

import jax
import jax.numpy as jnp
from jax import lax
from jax.experimental import pallas as pl
from jax.experimental.pallas import tpu as pltpu
from jax.sharding import PartitionSpec as P

HDIM = 128
RATIO = 4
MESH = pl.DeviceIdType.MESH
ANY = pl.BlockSpec(memory_space=pl.ANY)


def rms_scale(values_in):
    return values_in * lax.rsqrt(jnp.mean(values_in * values_in, -1, keepdims=True) + 1e-06)


def plane_width(seq_count):
    return 2 if seq_count % 2 == 0 else 1


LANES = 128
VMEM = pl.BlockSpec(memory_space=pltpu.VMEM)


def remote(source, target, send, recv, device):
    return pltpu.make_async_remote_copy(
        src_ref=source, dst_ref=target, send_sem=send, recv_sem=recv,
        device_id=device, device_id_type=MESH,
    )


def to_column(row):
    return jnp.transpose(jnp.broadcast_to(row, (LANES, row.shape[1])))[:, :1]


class Grid:
    def __init__(self, seq_count, head_count):
        self.wide = plane_width(seq_count)
        self.heads = head_count
        self.cores = 2 if head_count % 2 == 0 else 1
        self.length = seq_count // self.wide
        self.size = self.wide * head_count
        self.dims = (self.wide, head_count // self.cores, self.cores)
        seq, head = lax.axis_index("seq"), lax.axis_index("head")
        self.z, self.y = seq // self.wide, lax.rem(seq, self.wide)
        self.x, self.c = head // self.cores, lax.rem(head, self.cores)
        self.me = self.place(self.y, self.x, self.c)
        turns = [
            (ky, kx, kc)
            for ky in range(self.dims[0]) for kx in range(self.dims[1]) for kc in range(self.dims[2])
        ]
        self.turns = sorted(turns[1:], key=lambda turn: (turn[0] + turn[1], turn))
        self.chips = [turn for turn in self.turns if turn[2] == 0]

    def place(self, y, x, c):
        return (y * self.dims[1] + x) * self.cores + c

    def shifted(self, turn, sign):
        at = (self.y, self.x, self.c)
        return [lax.rem(at[i] + (sign * turn[i] + self.dims[i]), self.dims[i]) for i in range(3)]

    def to(self, turn):
        y, x, c = self.shifted(turn, 1)
        return self.place(y, x, c), self.device(self.z, y, x, c), y

    def source(self, turn):
        return self.place(*self.shifted(turn, -1))

    def device(self, z, y, x, c):
        return (z * self.wide + y, x * self.cores + c)

    def along(self, z):
        return self.device(z, self.y, self.x, self.c)

    def sibling(self):
        return self.device(self.z, self.y, self.x, lax.rem(self.c + 1, 2))

    def greet(self):
        barrier = pltpu.get_barrier_semaphore()
        last = self.length - 1

        def hail(device):
            pl.semaphore_signal(barrier, inc=1, device_id=device, device_id_type=MESH)

        for turn in self.turns:
            hail(self.to(turn)[1])

        count = len(self.turns)
        for off in (-2, -1, 1, 2):
            there = (self.z + off >= 0) & (self.z + off <= last)
            count = count + jnp.where(there, 1, 0)

            @pl.when(there)
            def _():
                hail(self.along(self.z + off))

        pl.semaphore_wait(barrier, count)


def steps(count, body, reverse=False):
    if count <= 8:
        for number in reversed(range(count)) if reverse else range(count):
            body(number)
    else:
        def one(number, carry):
            body(count - 1 - number if reverse else number)
            return carry
        lax.fori_loop(0, count, one, 0)


def front_kernel(
    seq_count, head_count, chunks, cached, tokens, owners, slots, gain, shift, normed, all_ids, seen,
    far, far_ids, hot, hot_far, part, passing, skip, raw, id_send, id_recv, far_id_send,
    far_id_recv, seen_send, seen_recv, own_sem, far_send, far_recv, pass_send, pass_recv,
    skip_send, skip_recv, raw_send, raw_recv, twin_send, twin_recv,
    early=lambda: None, meanwhile=lambda: None,
):
    grid = Grid(seq_count, head_count)
    z, me, length = grid.z, grid.me, grid.length
    src_rows = tokens.shape[0]
    rows = part.shape[2]
    merged_rows = rows // grid.wide
    width = chunks * LANES
    feature_width = width * grid.size
    low = z < (length + 1) // 2
    sign = jnp.where(low, 1, -1)
    home = jnp.where(low, z, length - 1 - z)
    inward = jnp.where(low, 1, 0)
    outward = 1 - inward
    at_end, near = home == 0, home == 1

    def slab(index, chunk):
        return pl.ds(pl.multiple_of(index * width + chunk * LANES, LANES), LANES)

    all_ids[me] = owners[...] * merged_rows + slots[...]
    grid.greet()
    id_copies, seen_copies, owns = [], [], []
    for step, turn in enumerate(grid.turns):
        copy = remote(all_ids.at[me], all_ids.at[me], id_send.at[step], id_recv.at[step], grid.to(turn)[1])
        copy.start()
        id_copies.append(copy)
    for chunk in range(chunks):
        own = pltpu.make_async_copy(tokens.at[:, slab(me, chunk)], seen.at[chunk, me], own_sem.at[chunk])
        own.start()
        owns.append(own)
        copies = []
        for step, turn in enumerate(grid.turns):
            index, device, _ = grid.to(turn)
            copy = remote(tokens.at[:, slab(index, chunk)], seen.at[chunk, me],
                          seen_send.at[chunk, step], seen_recv.at[chunk, step], device)
            copy.start()
            copies.append(copy)
        seen_copies.append(copies)
    early()

    def far_block(chunk, index):
        return remote(seen.at[chunk, index], far.at[chunk, index], far_send.at[chunk],
                      far_recv.at[chunk], grid.along(z + sign))

    def far_whole(chunk):
        return remote(seen.at[chunk], far.at[chunk], far_send.at[chunk], far_recv.at[chunk],
                      grid.along(z + sign))

    far_names = remote(all_ids, far_ids, far_id_send, far_id_recv, grid.along(z + sign))
    for copy in id_copies:
        copy.wait_recv()

    @pl.when(at_end)
    def _():
        far_names.start()

    places = lax.broadcasted_iota(jnp.int32, (rows, 1), 0)

    def marks(names, dest):
        labels = jnp.concatenate([names[index] for index in range(grid.size)], axis=1)
        return (places + dest * rows == labels).astype(jnp.float32).astype(jnp.bfloat16)

    def summed(chunk, dest):
        chosen = hot[dest] if cached else marks(all_ids, dest)
        return jnp.dot(chosen, seen[chunk].reshape(grid.size * src_rows, LANES),
                       preferred_element_type=jnp.float32)

    def summed_far(chunk, dest):
        chosen = hot_far[dest] if cached else marks(far_ids, dest)
        return jnp.dot(chosen, far[chunk].reshape(grid.size * src_rows, LANES),
                       preferred_element_type=jnp.float32)

    @pl.when(at_end)
    def _():
        def begin(chunk):
            owns[chunk].wait()
            far_block(chunk, me).start()

        def follow(chunk, step):
            seen_copies[chunk][step].wait_recv()
            far_block(chunk, grid.source(grid.turns[step])).start()

        for chunk in range(min(2, chunks)):
            begin(chunk)
            follow(chunk, 0)
        for chunk in range(chunks):
            if chunk > 1:
                begin(chunk)
                follow(chunk, 0)
            for step in range(1, len(grid.turns)):
                follow(chunk, step)
        if cached:
            hot[z] = marks(all_ids, z)
        for chunk in range(chunks):
            part[chunk, z] = summed(chunk, z)

    @pl.when(jnp.logical_not(at_end))
    def _():
        if cached:
            for dest in range(length):
                hot[dest] = marks(all_ids, dest)

        @pl.when(near)
        def _():
            far_names.wait_recv()
            if cached:
                for dest in range(length):
                    hot_far[dest] = marks(far_ids, dest)

    meanwhile()

    def block_rows(ky):
        y = lax.rem(grid.y + ky, grid.wide)
        return pl.ds(pl.multiple_of(y * merged_rows, merged_rows), merged_rows)

    order = list(reversed(range(grid.wide)))

    def hop(chunk, dest, direction, sense, ky):
        spot = dest + sense
        return remote(part.at[chunk, dest, block_rows(ky)], passing.at[chunk, spot, block_rows(ky)],
                      pass_send.at[chunk, spot, ky], pass_recv.at[chunk, spot, ky],
                      grid.along(z + direction))

    def leap(chunk, dest, direction, sense, ky):
        return remote(part.at[chunk, dest, block_rows(ky)], skip.at[chunk, sense, block_rows(ky)],
                      skip_send.at[chunk, sense, ky], skip_recv.at[chunk, sense, ky],
                      grid.along(z + 2 * direction))

    def send(chunk, dest, direction, sense, far_off, act):
        for ky in order:
            for kind, here in ((leap, far_off == 2), (hop, far_off != 2)):
                def one():
                    act(kind(chunk, dest, direction, sense, ky))
                if isinstance(far_off, int):
                    if here:
                        one()
                else:
                    pl.when(here)(one)

    def add_passing(chunk, dest, direction, sense):
        for ky in order:
            hop(chunk, dest, direction, sense, ky).wait_recv()
        part[chunk, dest] += passing[chunk, dest + sense]

    def go_now(copy):
        copy.start()

    def away(chunk):
        def one(back):
            far_off = back + 1

            @pl.when(far_off <= length - 1 - home)
            def _():
                dest = z + sign * far_off
                part[chunk, dest] = summed(chunk, dest)

                @pl.when(near)
                def _():
                    part[chunk, dest] += summed_far(chunk, dest)

                @pl.when((home >= 2) & (far_off > 1))
                def _():
                    add_passing(chunk, dest, sign, inward)

                send(chunk, dest, sign, inward, far_off, go_now)

        steps(length - 1, one, reverse=True)
        part[chunk, z] = summed(chunk, z)

        @pl.when(near)
        def _():
            part[chunk, z] += summed_far(chunk, z)

    def home_next(chunk):
        part[chunk, z - sign] = summed(chunk, z - sign)
        send(chunk, z - sign, -sign, outward, 1, go_now)

    def home_far(chunk):
        def one(back):
            far_off = back + 2

            @pl.when(far_off <= home)
            def _():
                dest = z - sign * far_off
                part[chunk, dest] = summed(chunk, dest)
                add_passing(chunk, dest, -sign, outward)
                send(chunk, dest, -sign, outward, far_off, go_now)

        steps(max((length + 1) // 2 - 2, 0), one, reverse=True)

    raw_copies, twin_copies = [], []

    def finish(chunk):
        copies, twins = [None] * len(grid.chips), []
        raw_copies.append(copies)
        twin_copies.append(twins)
        for ky in order:
            where = block_rows(ky)
            sources = [
                (home >= 2, hop, passing, z + inward, sign, inward),
                (home >= 3, leap, skip, inward, sign, inward),
                (home >= 0, hop, passing, z + outward, -sign, outward),
                (home + 2 <= length - 2, leap, skip, outward, -sign, outward),
            ]
            for there, kind, buffer, spot, direction, sense in sources:
                @pl.when(there)
                def _():
                    kind(chunk, z, direction, sense, ky).wait_recv()
                    part[chunk, z, where] += buffer[chunk, spot, where]

            for step, turn in enumerate(grid.chips):
                if turn[0] == ky:
                    copy = remote(part.at[chunk, z, where], raw.at[me * chunks + chunk],
                                  raw_send.at[chunk, step], raw_recv.at[chunk, step], grid.to(turn)[1])
                    copy.start()
                    copies[step] = copy
            if ky == 0:
                raw[me * chunks + chunk] = part[chunk, z, where]
                hand_over(chunk, me, len(grid.chips))

    def hand_over(chunk, index, step):
        if grid.cores == 1:
            return
        spot = raw.at[index * chunks + chunk]
        copy = remote(spot, spot, twin_send.at[chunk, step], twin_recv.at[chunk, step], grid.sibling())
        copy.start()
        twin_copies[chunk].append(copy)

    def pass_over(chunk):
        for step, turn in enumerate(grid.chips):
            raw_copies[chunk][step].wait_recv()
            hand_over(chunk, grid.source(turn), step)

    for chunk in range(chunks):
        @pl.when(jnp.logical_not(at_end))
        def _():
            owns[chunk].wait()
            for copy in seen_copies[chunk]:
                copy.wait_recv()
            home_next(chunk)

            @pl.when(near)
            def _():
                far_whole(chunk).wait_recv()

            away(chunk)

        if chunk > 0:
            finish(chunk - 1)
        if chunk > 1:
            pass_over(chunk - 2)

        @pl.when(jnp.logical_not(at_end))
        def _():
            home_far(chunk)

    finish(chunks - 1)
    for chunk in range(max(chunks - 2, 0), chunks):
        pass_over(chunk)
    for copies in twin_copies:
        for copy in copies:
            copy.wait_recv()
    blocks = grid.size * chunks
    acc = raw[0]
    for block in range(1, blocks):
        acc += raw[block]
    mean = jnp.sum(acc, -1, keepdims=True) * (1.0 / feature_width)
    acc = jnp.zeros_like(acc)
    for block in range(blocks):
        apart = raw[block] - mean
        acc += apart * apart
    scale = lax.rsqrt(jnp.sum(acc, -1, keepdims=True) * (1.0 / feature_width) + 1e-06)
    for block in range(blocks):
        spot = slice(block * LANES, (block + 1) * LANES)
        normed[:, spot] = ((raw[block] - mean) * scale * gain[:, spot] + shift[:, spot]).astype(jnp.bfloat16)

    def done(copy):
        copy.wait_send()

    for copy in id_copies:
        copy.wait_send()
    for chunk in range(chunks):
        for copy in seen_copies[chunk] + raw_copies[chunk] + twin_copies[chunk]:
            copy.wait_send()

    @pl.when(at_end)
    def _():
        far_names.wait_send()
        for chunk in range(chunks):
            far_whole(chunk).wait_send()

    @pl.when(jnp.logical_not(at_end))
    def _():
        for chunk in range(chunks):
            def sent(number):
                far_off = number + 1

                @pl.when(far_off <= length - 1 - home)
                def _():
                    send(chunk, z + sign * far_off, sign, inward, far_off, done)

                @pl.when(far_off <= home)
                def _():
                    send(chunk, z - sign * far_off, -sign, outward, far_off, done)

            steps(length - 1, sent)


def weight_loads(heads, w_qkv, w_out, w_pair, w_query, w_last, load_sem):
    loads = []
    for head in range(heads):
        for kind in range(2):
            loads.append(pltpu.make_async_copy(
                w_qkv.at[kind + 1, :, pl.ds(head * HDIM, HDIM)],
                w_pair.at[head, :, pl.ds(kind * HDIM, HDIM)], load_sem.at[head, kind]))
    load_query = pltpu.make_async_copy(w_qkv.at[0], w_query, load_sem.at[heads, 0])
    load_last = pltpu.make_async_copy(w_out, w_last, load_sem.at[heads, 1])
    return loads, load_query, load_last


def fill_chooser(ids, chooser):
    size, src_rows = ids.shape[0], ids.shape[2]
    places = lax.broadcasted_iota(jnp.int32, (1, chooser.shape[1]), 1)
    for index in range(size):
        chooser[index * src_rows:(index + 1) * src_rows] = (
            (to_column(ids[index]) == places).astype(jnp.float32).astype(jnp.bfloat16)
        )


def rest_kernel(
    seq_count, head_count, chunks, heads, normed, w_qkv, w_out, query_gain, key_gain, gate, ids, out,
    w_pair, w_query, w_last, pairs, queries, chooser, theirs, came, mine, leaving, pieces, merged, fetched,
    load_sem, ring_send, ring_recv, twin_send, twin_recv, piece_send, piece_recv, up_send, up_recv,
    down_send, down_recv, back_send, back_recv, fused=False,
):
    grid = Grid(seq_count, head_count)
    z, me, length = grid.z, grid.me, grid.length
    src_rows = out.shape[0]
    merged_rows = normed.shape[0]
    rows = merged.shape[2]
    width = chunks * LANES
    half = seq_count // 2
    spot_in_ring = jnp.where(grid.y == 0, z, seq_count - 1 - z)

    def ring_device(position):
        position = lax.rem(position + seq_count, seq_count)
        low = position < length
        return grid.device(jnp.where(low, position, seq_count - 1 - position),
                           jnp.where(low, 0, 1), grid.x, grid.c)

    def slab(index, chunk):
        return pl.ds(pl.multiple_of(index * width + chunk * LANES, LANES), LANES)

    loads, load_query, load_last = weight_loads(heads, w_qkv, w_out, w_pair, w_query, w_last, load_sem)
    if not fused:
        for load in loads + [load_query, load_last]:
            load.start()
        grid.greet()

    def ring_copy(way, kind, head, step):
        sign = 1 - 2 * way
        origin = lax.rem(spot_in_ring - sign * (step - 1) + 2 * seq_count, seq_count)
        block = pairs.at[head, origin, kind]
        return remote(block, block, ring_send.at[way, kind, head, step - 1],
                      ring_recv.at[way, kind, head, step - 1], ring_device(spot_in_ring + sign))

    def reach(way, kind):
        return half if way == kind else half - 1

    lines = [(way, kind) for kind in range(2) for way in range(2)]
    for head in range(heads):
        loads[2 * head].wait()
        loads[2 * head + 1].wait()
        made = jnp.dot(normed[...], w_pair[head], preferred_element_type=jnp.float32)
        pairs[head, spot_in_ring, 0] = (rms_scale(made[:, :HDIM]) * key_gain[...]).astype(jnp.bfloat16)
        pairs[head, spot_in_ring, 1] = made[:, HDIM:].astype(jnp.bfloat16)
        for way, kind in lines:
            ring_copy(way, kind, head, 1).start()
    load_query.wait()
    made = jnp.dot(normed[...], w_query[...], preferred_element_type=jnp.float32)
    for head in range(heads):
        one = made[:, head * HDIM:(head + 1) * HDIM]
        queries[head] = (rms_scale(one) * (query_gain[...] / math.sqrt(HDIM))).astype(jnp.bfloat16)
    if not fused:
        fill_chooser(ids, chooser)

    def pass_round(back):
        step = back + 1
        for head in range(heads):
            for way, kind in lines:
                ring_copy(way, kind, head, step).wait_recv()

                if reach(way, kind) == half:
                    ring_copy(way, kind, head, step + 1).start()
                else:
                    @pl.when(step < half - 1)
                    def _():
                        ring_copy(way, kind, head, step + 1).start()

    steps(half - 1, pass_round)
    load_last.wait()
    attended = []
    for head in range(heads):
        for kind in range(2):
            ring_copy(kind, kind, head, half).wait_recv()
        keys = pairs[head, :, 0].reshape(-1, HDIM)
        values = pairs[head, :, 1].reshape(-1, HDIM)
        scores = lax.dot_general(
            queries[head], keys, (((1,), (1,)), ((), ())), preferred_element_type=jnp.float32
        )
        expo = jnp.exp(scores - jnp.max(scores, -1, keepdims=True))
        total = jnp.sum(expo, -1, keepdims=True)
        weighted = jnp.dot(expo.astype(jnp.bfloat16), values, preferred_element_type=jnp.float32)
        attended.append((weighted / total).astype(jnp.bfloat16))
    attended = jnp.concatenate(attended, axis=1)

    spots = [(0, 0, 0)] + grid.chips
    twin_copies = []

    def product(turn, flip):
        y, x, c = grid.shifted(turn, 1)
        if flip:
            c = lax.rem(c + 1, grid.cores)
        start = pl.multiple_of(grid.place(y, x, c) * width, LANES)
        return jnp.dot(attended, w_last[:, pl.ds(start, width)], preferred_element_type=jnp.float32)

    for number, turn in enumerate(spots):
        theirs[number] = product(turn, True)
        copy = remote(theirs.at[number], came.at[number], twin_send.at[number], twin_recv.at[number],
                      grid.sibling())
        copy.start()
        twin_copies.append(copy)
    for number, turn in enumerate(spots):
        mine[number] = product(turn, False)
    for number in range(len(spots)):
        twin_copies[number].wait_recv()
        mine[number] += came[number]
    started, piece_copies = [], []

    def go(copy):
        copy.start()
        started.append(copy)
        return copy

    for chunk in range(chunks):
        copies = []
        for step, turn in enumerate(grid.chips):
            leaving[chunk, step] = mine[step + 1, :, chunk * LANES:(chunk + 1) * LANES].astype(jnp.bfloat16)
            copies.append(go(remote(
                leaving.at[chunk, step], pieces.at[chunk, step], piece_send.at[chunk, step],
                piece_recv.at[chunk, step], grid.to(turn)[1])))
        piece_copies.append(copies)

    def collect(chunk):
        for copy in piece_copies[chunk]:
            copy.wait_recv()
        for ky in range(grid.wide):
            total = mine[0, :, chunk * LANES:(chunk + 1) * LANES] if ky == 0 else None
            for step, turn in enumerate(grid.chips):
                if turn[0] == ky:
                    piece = pieces[chunk, step].astype(jnp.float32)
                    total = piece if total is None else total + piece
            y = lax.rem(grid.y - ky + grid.wide, grid.wide)
            merged[chunk, z, pl.ds(pl.multiple_of(y * merged_rows, merged_rows), merged_rows)] = (
                total * gate[:, slab(me, chunk)]
            ).astype(jnp.bfloat16)

    def upward(chunk, far):
        spot = merged.at[chunk, z - far]
        return remote(spot, spot, up_send.at[chunk, far], up_recv.at[chunk, far], grid.along(z + 1))

    def downward(chunk, far):
        spot = merged.at[chunk, z + far]
        return remote(spot, spot, down_send.at[chunk, far], down_recv.at[chunk, far], grid.along(z - 1))

    def came_up(chunk, far):
        spot = merged.at[chunk, z - far]
        return remote(spot, spot, up_send.at[chunk, far - 1], up_recv.at[chunk, far - 1], grid.along(z + 1))

    def came_down(chunk, far):
        spot = merged.at[chunk, z + far]
        return remote(spot, spot, down_send.at[chunk, far - 1], down_recv.at[chunk, far - 1],
                      grid.along(z - 1))

    def pass_on(chunk, far):
        if far < length - 1:
            @pl.when((z >= far) & (z < length - 1))
            def _():
                upward(chunk, far).start()

            @pl.when((z + far < length) & (z > 0))
            def _():
                downward(chunk, far).start()

    back_copies = []
    for round_number in range(chunks + length - 1):
        for far in range(length):
            chunk = round_number - far
            if not 0 <= chunk < chunks:
                continue
            if far == 0:
                collect(chunk)
            else:
                @pl.when(z >= far)
                def _():
                    came_up(chunk, far).wait_recv()

                @pl.when(z + far < length)
                def _():
                    came_down(chunk, far).wait_recv()
            pass_on(chunk, far)
            if far == length - 1:
                fetched[chunk] = (
                    jnp.dot(
                        chooser[...],
                        merged[chunk].reshape(length * rows, LANES),
                        preferred_element_type=jnp.float32,
                    )
                    .astype(jnp.bfloat16)
                    .reshape(grid.size, src_rows, LANES)
                )
                for step, turn in enumerate(grid.turns):
                    index, device, _ = grid.to(turn)
                    back_copies.append(go(remote(
                        fetched.at[chunk, index], out.at[:, slab(me, chunk)], back_send.at[chunk, step],
                        back_recv.at[chunk, step], device)))
                out[:, slab(me, chunk)] = fetched[chunk, me]
    for head in range(heads):
        for way, kind in lines:
            def sent(back):
                ring_copy(way, kind, head, back + 1).wait_send()

            steps(reach(way, kind), sent)
    for copy in twin_copies:
        copy.wait_send()
    for chunk in range(chunks):
        for far in range(length - 1):
            @pl.when((z >= far) & (z < length - 1))
            def _():
                upward(chunk, far).wait_send()

            @pl.when((z + far < length) & (z > 0))
            def _():
                downward(chunk, far).wait_send()
    for copy in back_copies:
        copy.wait_recv()
    for copy in started:
        copy.wait_send()


def sublayer(tokens, owners, slots, w_qkv, w_out, norm_gain, norm_shift, query_gain, key_gain, out_gate):
    seq_count, head_count = lax.axis_size("seq"), lax.axis_size("head")
    wide = plane_width(seq_count)
    length, size = seq_count // wide, wide * head_count
    src_rows, feature_width = tokens.shape
    width = feature_width // size
    chunks = width // LANES
    merged_rows = src_rows * head_count // RATIO
    rows, labels = wide * merged_rows, size * src_rows
    inner = w_qkv.shape[2]
    heads = inner // HDIM
    cached = length * rows * labels * 4 <= 8 * 2**20
    marks_shape = (length, rows, labels) if cached else (1, 16, LANES)
    dma, turns, spots, half = pltpu.SemaphoreType.DMA, size - 1, size // 2, seq_count // 2
    normed = jax.ShapeDtypeStruct((merged_rows, feature_width), jnp.bfloat16)
    names = jax.ShapeDtypeStruct((size, 1, src_rows), jnp.int32)
    result = jax.ShapeDtypeStruct((src_rows, feature_width), jnp.bfloat16)
    front_scratch = [
        pltpu.VMEM((chunks, size, src_rows, LANES), jnp.bfloat16),
        pltpu.VMEM((chunks, size, src_rows, LANES), jnp.bfloat16),
        pltpu.VMEM((size, 1, src_rows), jnp.int32),
        pltpu.VMEM(marks_shape, jnp.bfloat16),
        pltpu.VMEM(marks_shape, jnp.bfloat16),
        pltpu.VMEM((chunks, length, rows, LANES), jnp.float32),
        pltpu.VMEM((chunks, length + 1, rows, LANES), jnp.float32),
        pltpu.VMEM((chunks, 2, rows, LANES), jnp.float32),
        pltpu.VMEM((size * chunks, merged_rows, LANES), jnp.float32),
        dma((turns,)),
        dma((turns,)),
        dma(()),
        dma(()),
        dma((chunks, turns)),
        dma((chunks, turns)),
        dma((chunks,)),
        dma((chunks,)),
        dma((chunks,)),
        dma((chunks, length + 1, wide)),
        dma((chunks, length + 1, wide)),
        dma((chunks, 2, wide)),
        dma((chunks, 2, wide)),
        dma((chunks, spots)),
        dma((chunks, spots)),
        dma((chunks, spots)),
        dma((chunks, spots)),
    ]
    rest_scratch = [
        pltpu.VMEM((heads, feature_width, 2 * HDIM), jnp.bfloat16),
        pltpu.VMEM((feature_width, inner), jnp.bfloat16),
        pltpu.VMEM((inner, feature_width), jnp.bfloat16),
        pltpu.VMEM((heads, seq_count, 2, merged_rows, HDIM), jnp.bfloat16),
        pltpu.VMEM((heads, merged_rows, HDIM), jnp.bfloat16),
        pltpu.VMEM((labels, length * rows), jnp.bfloat16),
        pltpu.VMEM((spots, merged_rows, width), jnp.float32),
        pltpu.VMEM((spots, merged_rows, width), jnp.float32),
        pltpu.VMEM((spots, merged_rows, width), jnp.float32),
        pltpu.VMEM((chunks, spots, merged_rows, LANES), jnp.bfloat16),
        pltpu.VMEM((chunks, spots, merged_rows, LANES), jnp.bfloat16),
        pltpu.VMEM((chunks, length, rows, LANES), jnp.bfloat16),
        pltpu.VMEM((chunks, size, src_rows, LANES), jnp.bfloat16),
        dma((heads + 1, 2)),
        dma((2, 2, heads, half)),
        dma((2, 2, heads, half)),
        dma((spots,)),
        dma((spots,)),
        dma((chunks, spots)),
        dma((chunks, spots)),
        dma((chunks, length)),
        dma((chunks, length)),
        dma((chunks, length)),
        dma((chunks, length)),
        dma((chunks, turns)),
        dma((chunks, turns)),
    ]
    front_body = functools.partial(front_kernel, seq_count, head_count, chunks, cached)
    rest_body = functools.partial(rest_kernel, seq_count, head_count, chunks, heads)

    def call(name, number, body, out_shape, in_specs, scratch, arguments):
        return pl.pallas_call(
            body, out_shape=out_shape, in_specs=in_specs,
            out_specs=jax.tree.map(lambda _: VMEM, out_shape), scratch_shapes=scratch,
            compiler_params=pltpu.CompilerParams(
                collective_id=number, has_side_effects=True, vmem_limit_bytes=60 * 2**20
            ),
            name=name,
        )(*arguments)

    fused = length * rows * labels <= 2 * 2**20
    if not fused:
        made, ids = call("front", 0, front_body, [normed, names], [ANY] + [VMEM] * 4, front_scratch,
                         (tokens, owners, slots, norm_gain, norm_shift))
        return call("rest", 1, rest_body, result, [VMEM, ANY, ANY] + [VMEM] * 4, rest_scratch,
                    (made, w_qkv, w_out, query_gain, key_gain, out_gate, ids))

    def whole_kernel(*refs):
        front_in, rest_in, out = refs[:5], refs[5:10], refs[10]
        made, ids = refs[11:13]
        front_refs = refs[13:13 + len(front_scratch)]
        rest_refs = refs[13 + len(front_scratch):]
        loads, load_query, load_last = weight_loads(heads, *rest_in[:2], *rest_refs[:3], rest_refs[13])

        def start_loads():
            for load in loads + [load_query, load_last]:
                load.start()

        front_body(*front_in, made, ids, *front_refs, early=start_loads,
                   meanwhile=lambda: fill_chooser(ids, rest_refs[5]))
        rest_body(made, *rest_in, ids, out, *rest_refs, fused=True)

    kept = [pltpu.VMEM(normed.shape, normed.dtype), pltpu.VMEM(names.shape, names.dtype)]
    return call("sublayer", 2, whole_kernel, result, [ANY] + [VMEM] * 4 + [ANY] * 2 + [VMEM] * 3,
                kept + front_scratch + rest_scratch,
                (tokens, owners, slots, norm_gain, norm_shift, w_qkv, w_out, query_gain, key_gain,
                 out_gate))


def on_device(
    tokens,
    owner_shard,
    dest_slot,
    w_qkv,
    w_out,
    norm_gain,
    norm_shift,
    query_gain,
    key_gain,
    out_gate,
):
    return sublayer(tokens, owner_shard.T, dest_slot[None], jnp.transpose(w_qkv, (1, 0, 2)), w_out,
                    norm_gain[None], norm_shift[None], query_gain[None], key_gain[None], out_gate[None])


def solution(mesh):
    placed = (
        P(("seq", "head"), None),
        P(("seq", "head"), None),
        P(("seq", "head")),
        P(None, None, "head"),
        P("head", None),
        P(),
        P(),
        P(),
        P(),
        P(),
    )
    return jax.shard_map(
        on_device, mesh=mesh, in_specs=placed, out_specs=P(("seq", "head"), None), check_vma=False
    )
```

```python
import functools
import math

import jax
import jax.numpy as jnp
from jax import lax
from jax.experimental import pallas as pl
from jax.experimental.pallas import tpu as pltpu
from jax.sharding import PartitionSpec as P

HDIM = 128
RATIO = 4
MESH = pl.DeviceIdType.MESH
ANY = pl.BlockSpec(memory_space=pl.ANY)


def rms_scale(values_in):
    return values_in * lax.rsqrt(jnp.mean(values_in * values_in, -1, keepdims=True) + 1e-06)


def plane_width(seq_count):
    return 2 if seq_count % 2 == 0 else 1


LANES = 128
VMEM = pl.BlockSpec(memory_space=pltpu.VMEM)


def remote(source, target, send, recv, device):
    return pltpu.make_async_remote_copy(
        src_ref=source, dst_ref=target, send_sem=send, recv_sem=recv,
        device_id=device, device_id_type=MESH,
    )


def to_column(row):
    return jnp.transpose(jnp.broadcast_to(row, (LANES, row.shape[1])))[:, :1]


class Grid:
    def __init__(self, seq_count, head_count):
        self.wide = plane_width(seq_count)
        self.heads = head_count
        self.cores = 2 if head_count % 2 == 0 else 1
        self.length = seq_count // self.wide
        self.size = self.wide * head_count
        self.dims = (self.wide, head_count // self.cores, self.cores)
        seq, head = lax.axis_index("seq"), lax.axis_index("head")
        self.z, self.y = seq // self.wide, lax.rem(seq, self.wide)
        self.x, self.c = head // self.cores, lax.rem(head, self.cores)
        self.me = self.place(self.y, self.x, self.c)
        turns = [
            (ky, kx, kc)
            for ky in range(self.dims[0]) for kx in range(self.dims[1]) for kc in range(self.dims[2])
        ]
        self.turns = sorted(turns[1:], key=lambda turn: (turn[0] + turn[1], turn))
        self.chips = [turn for turn in self.turns if turn[2] == 0]

    def place(self, y, x, c):
        return (y * self.dims[1] + x) * self.cores + c

    def shifted(self, turn, sign):
        at = (self.y, self.x, self.c)
        return [lax.rem(at[i] + (sign * turn[i] + self.dims[i]), self.dims[i]) for i in range(3)]

    def to(self, turn):
        y, x, c = self.shifted(turn, 1)
        return self.place(y, x, c), self.device(self.z, y, x, c), y

    def source(self, turn):
        return self.place(*self.shifted(turn, -1))

    def device(self, z, y, x, c):
        return (z * self.wide + y, x * self.cores + c)

    def along(self, z):
        return self.device(z, self.y, self.x, self.c)

    def sibling(self):
        return self.device(self.z, self.y, self.x, lax.rem(self.c + 1, 2))

    def greet(self):
        barrier = pltpu.get_barrier_semaphore()
        last = self.length - 1

        def hail(device):
            pl.semaphore_signal(barrier, inc=1, device_id=device, device_id_type=MESH)

        for turn in self.turns:
            hail(self.to(turn)[1])

        count = len(self.turns)
        for off in (-2, -1, 1, 2):
            there = (self.z + off >= 0) & (self.z + off <= last)
            count = count + jnp.where(there, 1, 0)

            @pl.when(there)
            def _():
                hail(self.along(self.z + off))

        pl.semaphore_wait(barrier, count)


def steps(count, body, reverse=False):
    if count <= 8:
        for number in reversed(range(count)) if reverse else range(count):
            body(number)
    else:
        def one(number, carry):
            body(count - 1 - number if reverse else number)
            return carry
        lax.fori_loop(0, count, one, 0)


def front_kernel(
    seq_count, head_count, chunks, cached, tokens, owners, slots, gain, shift, normed, all_ids, seen,
    far, far_ids, hot, hot_far, part, passing, skip, raw, id_send, id_recv, far_id_send,
    far_id_recv, seen_send, seen_recv, own_sem, far_send, far_recv, pass_send, pass_recv,
    skip_send, skip_recv, raw_send, raw_recv, twin_send, twin_recv, turn_sem,
    early=lambda: None, meanwhile=lambda: None,
):
    grid = Grid(seq_count, head_count)
    z, me, length = grid.z, grid.me, grid.length
    src_rows = tokens.shape[0]
    rows = part.shape[2]
    merged_rows = rows // grid.wide
    width = chunks * LANES
    feature_width = width * grid.size
    low = z < (length + 1) // 2
    sign = jnp.where(low, 1, -1)
    home = jnp.where(low, z, length - 1 - z)
    inward = jnp.where(low, 1, 0)
    outward = 1 - inward
    at_end, near = home == 0, home == 1

    def slab(index, chunk):
        return pl.ds(pl.multiple_of(index * width + chunk * LANES, LANES), LANES)

    all_ids[me] = owners[...] * merged_rows + slots[...]
    grid.greet()
    id_copies, seen_copies, owns = [], [], []
    for step, turn in enumerate(grid.turns):
        copy = remote(all_ids.at[me], all_ids.at[me], id_send.at[step], id_recv.at[step], grid.to(turn)[1])
        copy.start()
        id_copies.append(copy)
    for chunk in range(chunks):
        own = pltpu.make_async_copy(tokens.at[:, slab(me, chunk)], seen.at[chunk, me], own_sem.at[chunk])
        own.start()
        owns.append(own)
        copies = []
        for step, turn in enumerate(grid.turns):
            index, device, _ = grid.to(turn)
            copy = remote(tokens.at[:, slab(index, chunk)], seen.at[chunk, me],
                          seen_send.at[chunk, step], seen_recv.at[chunk, step], device)
            copies.append(copy)
        seen_copies.append(copies)
    for core in range(grid.cores):
        @pl.when(grid.c == core)
        def _():
            for chunk in range(chunks):
                for target in range(grid.cores):
                    for step, turn in enumerate(grid.turns):
                        if (core + turn[2]) % grid.cores == target:
                            seen_copies[chunk][step].start()
    early()

    def far_block(chunk, index, part_number):
        return remote(seen.at[chunk, index], far.at[chunk, index], far_send.at[chunk, part_number],
                      far_recv.at[chunk], grid.along(z + sign))

    def far_half(chunk, part_number):
        blocks = pl.ds(0, grid.size // 2)
        return remote(seen.at[chunk, blocks], far.at[chunk, blocks], far_send.at[chunk, part_number],
                      far_recv.at[chunk], grid.along(z + sign))

    def far_whole(chunk):
        return remote(seen.at[chunk], far.at[chunk], far_send.at[chunk, 0], far_recv.at[chunk],
                      grid.along(z + sign))

    far_names = remote(all_ids, far_ids, far_id_send, far_id_recv, grid.along(z + sign))
    for copy in id_copies:
        copy.wait_recv()

    @pl.when(at_end)
    def _():
        far_names.start()

    places = lax.broadcasted_iota(jnp.int32, (rows, 1), 0)

    def marks(names, dest):
        labels = jnp.concatenate([names[index] for index in range(grid.size)], axis=1)
        return (places + dest * rows == labels).astype(jnp.float32).astype(jnp.bfloat16)

    def summed(chunk, dest):
        chosen = hot[dest] if cached else marks(all_ids, dest)
        return jnp.dot(chosen, seen[chunk].reshape(grid.size * src_rows, LANES),
                       preferred_element_type=jnp.float32)

    def summed_far(chunk, dest):
        chosen = hot_far[dest] if cached else marks(far_ids, dest)
        return jnp.dot(chosen, far[chunk].reshape(grid.size * src_rows, LANES),
                       preferred_element_type=jnp.float32)

    def take_turn(chunk, after):
        if grid.cores == 1:
            return
        if after:
            @pl.when((grid.c == 0) | (chunk < chunks - 1))
            def _():
                pl.semaphore_signal(turn_sem, inc=1, device_id=grid.sibling(), device_id_type=MESH)
        else:
            @pl.when((grid.c == 1) | (chunk > 0))
            def _():
                pl.semaphore_wait(turn_sem, 1)

    @pl.when(at_end)
    def _():
        def begin(chunk):
            owns[chunk].wait()
            far_block(chunk, me, 0).start()

        def follow(chunk, step):
            seen_copies[chunk][step].wait_recv()
            far_block(chunk, grid.source(grid.turns[step]), (step + 1) // (grid.size // 2)).start()

        for chunk in range(chunks):
            take_turn(chunk, 0)
            begin(chunk)
            follow(chunk, 0)
            for step in range(1, len(grid.turns)):
                follow(chunk, step)
            far_half(chunk, 0).wait_send()
            take_turn(chunk, 1)
        if cached:
            hot[z] = marks(all_ids, z)
        for chunk in range(chunks):
            part[chunk, z] = summed(chunk, z)

    @pl.when(jnp.logical_not(at_end))
    def _():
        if cached:
            for dest in range(length):
                hot[dest] = marks(all_ids, dest)

        @pl.when(near)
        def _():
            far_names.wait_recv()
            if cached:
                for dest in range(length):
                    hot_far[dest] = marks(far_ids, dest)

    meanwhile()

    def block_rows(ky):
        y = lax.rem(grid.y + ky, grid.wide)
        return pl.ds(pl.multiple_of(y * merged_rows, merged_rows), merged_rows)

    order = list(reversed(range(grid.wide)))

    def hop(chunk, dest, direction, sense, ky):
        spot = dest + sense
        return remote(part.at[chunk, dest, block_rows(ky)], passing.at[chunk, spot, block_rows(ky)],
                      pass_send.at[chunk, spot, ky], pass_recv.at[chunk, spot, ky],
                      grid.along(z + direction))

    def leap(chunk, dest, direction, sense, ky):
        return remote(part.at[chunk, dest, block_rows(ky)], skip.at[chunk, sense, block_rows(ky)],
                      skip_send.at[chunk, sense, ky], skip_recv.at[chunk, sense, ky],
                      grid.along(z + 2 * direction))

    def send(chunk, dest, direction, sense, far_off, act):
        for ky in order:
            for kind, here in ((leap, far_off == 2), (hop, far_off != 2)):
                def one():
                    act(kind(chunk, dest, direction, sense, ky))
                if isinstance(far_off, int):
                    if here:
                        one()
                else:
                    pl.when(here)(one)

    def add_passing(chunk, dest, direction, sense):
        for ky in order:
            hop(chunk, dest, direction, sense, ky).wait_recv()
        part[chunk, dest] += passing[chunk, dest + sense]

    def go_now(copy):
        copy.start()

    def away(chunk):
        def one(back):
            far_off = back + 1

            @pl.when(far_off <= length - 1 - home)
            def _():
                dest = z + sign * far_off

                @pl.when(near)
                def _():
                    part[chunk, dest] += summed_far(chunk, dest)

                @pl.when((home >= 2) & (far_off > 1))
                def _():
                    add_passing(chunk, dest, sign, inward)

                send(chunk, dest, sign, inward, far_off, go_now)

        steps(length - 1, one, reverse=True)

        @pl.when(near)
        def _():
            part[chunk, z] += summed_far(chunk, z)

    def home_next(chunk):
        part[chunk, z - sign] = summed(chunk, z - sign)
        send(chunk, z - sign, -sign, outward, 1, go_now)

        def own(far_off):
            @pl.when(far_off <= length - 1 - home)
            def _():
                part[chunk, z + sign * far_off] = summed(chunk, z + sign * far_off)

        steps(length, own)

    def home_far(chunk):
        def one(back):
            far_off = back + 2

            @pl.when(far_off <= home)
            def _():
                dest = z - sign * far_off
                part[chunk, dest] = summed(chunk, dest)
                add_passing(chunk, dest, -sign, outward)
                send(chunk, dest, -sign, outward, far_off, go_now)

        steps(max((length + 1) // 2 - 2, 0), one, reverse=True)

    raw_copies, twin_copies = [], []

    def finish(chunk):
        copies, twins = [None] * len(grid.chips), []
        raw_copies.append(copies)
        twin_copies.append(twins)
        for ky in order:
            where = block_rows(ky)
            sources = [
                (home >= 2, hop, passing, z + inward, sign, inward),
                (home >= 3, leap, skip, inward, sign, inward),
                (home >= 0, hop, passing, z + outward, -sign, outward),
                (home + 2 <= length - 2, leap, skip, outward, -sign, outward),
            ]
            for there, kind, buffer, spot, direction, sense in sources:
                @pl.when(there)
                def _():
                    kind(chunk, z, direction, sense, ky).wait_recv()
                    part[chunk, z, where] += buffer[chunk, spot, where]

            for step, turn in enumerate(grid.chips):
                if turn[0] == ky:
                    copy = remote(part.at[chunk, z, where], raw.at[me * chunks + chunk],
                                  raw_send.at[chunk, step], raw_recv.at[chunk, step], grid.to(turn)[1])
                    copy.start()
                    copies[step] = copy
            if ky == 0:
                raw[me * chunks + chunk] = part[chunk, z, where]
                hand_over(chunk, me, len(grid.chips))

    def hand_over(chunk, index, step):
        if grid.cores == 1:
            return
        spot = raw.at[index * chunks + chunk]
        copy = remote(spot, spot, twin_send.at[chunk, step], twin_recv.at[chunk, step], grid.sibling())
        copy.start()
        twin_copies[chunk].append(copy)

    def pass_over(chunk):
        for step, turn in enumerate(grid.chips):
            raw_copies[chunk][step].wait_recv()
            hand_over(chunk, grid.source(turn), step)

    for chunk in range(chunks):
        @pl.when(jnp.logical_not(at_end))
        def _():
            owns[chunk].wait()
            for copy in seen_copies[chunk]:
                copy.wait_recv()
            home_next(chunk)

            @pl.when(near)
            def _():
                far_whole(chunk).wait_recv()

            away(chunk)

        if chunk > 0:
            finish(chunk - 1)
        if chunk > 1:
            pass_over(chunk - 2)

        @pl.when(jnp.logical_not(at_end))
        def _():
            home_far(chunk)

    finish(chunks - 1)
    for chunk in range(max(chunks - 2, 0), chunks):
        pass_over(chunk)
    for copies in twin_copies:
        for copy in copies:
            copy.wait_recv()
    blocks = grid.size * chunks
    acc = raw[0]
    for block in range(1, blocks):
        acc += raw[block]
    mean = jnp.sum(acc, -1, keepdims=True) * (1.0 / feature_width)
    acc = jnp.zeros_like(acc)
    for block in range(blocks):
        apart = raw[block] - mean
        acc += apart * apart
    scale = lax.rsqrt(jnp.sum(acc, -1, keepdims=True) * (1.0 / feature_width) + 1e-06)
    for block in range(blocks):
        spot = slice(block * LANES, (block + 1) * LANES)
        normed[:, spot] = ((raw[block] - mean) * scale * gain[:, spot] + shift[:, spot]).astype(jnp.bfloat16)

    def done(copy):
        copy.wait_send()

    for copy in id_copies:
        copy.wait_send()
    for chunk in range(chunks):
        for copy in seen_copies[chunk] + raw_copies[chunk] + twin_copies[chunk]:
            copy.wait_send()

    @pl.when(at_end)
    def _():
        far_names.wait_send()
        for chunk in range(chunks):
            far_half(chunk, 1).wait_send()

    @pl.when(jnp.logical_not(at_end))
    def _():
        for chunk in range(chunks):
            def sent(number):
                far_off = number + 1

                @pl.when(far_off <= length - 1 - home)
                def _():
                    send(chunk, z + sign * far_off, sign, inward, far_off, done)

                @pl.when(far_off <= home)
                def _():
                    send(chunk, z - sign * far_off, -sign, outward, far_off, done)

            steps(length - 1, sent)


def weight_loads(heads, w_qkv, w_out, w_pair, w_query, w_last, load_sem):
    loads = []
    for head in range(heads):
        for kind in range(2):
            loads.append(pltpu.make_async_copy(
                w_qkv.at[kind + 1, :, pl.ds(head * HDIM, HDIM)],
                w_pair.at[head, :, pl.ds(kind * HDIM, HDIM)], load_sem.at[head, kind]))
    load_query = pltpu.make_async_copy(w_qkv.at[0], w_query, load_sem.at[heads, 0])
    load_last = pltpu.make_async_copy(w_out, w_last, load_sem.at[heads, 1])
    return loads, load_query, load_last


def fill_chooser(ids, chooser):
    size, src_rows = ids.shape[0], ids.shape[2]
    places = lax.broadcasted_iota(jnp.int32, (1, chooser.shape[1]), 1)
    for index in range(size):
        chooser[index * src_rows:(index + 1) * src_rows] = (
            (to_column(ids[index]) == places).astype(jnp.float32).astype(jnp.bfloat16)
        )


def rest_kernel(
    seq_count, head_count, chunks, heads, normed, w_qkv, w_out, query_gain, key_gain, gate, ids, out,
    w_pair, w_query, w_last, pairs, queries, chooser, theirs, came, mine, leaving, pieces, merged, fetched,
    load_sem, ring_send, ring_recv, twin_send, twin_recv, piece_send, piece_recv, up_send, up_recv,
    down_send, down_recv, back_send, back_recv, keep_sem, fused=False,
):
    grid = Grid(seq_count, head_count)
    z, me, length = grid.z, grid.me, grid.length
    src_rows = out.shape[0]
    merged_rows = normed.shape[0]
    rows = merged.shape[2]
    width = chunks * LANES
    half = seq_count // 2
    spot_in_ring = jnp.where(grid.y == 0, z, seq_count - 1 - z)

    def ring_device(position):
        position = lax.rem(position + seq_count, seq_count)
        low = position < length
        return grid.device(jnp.where(low, position, seq_count - 1 - position),
                           jnp.where(low, 0, 1), grid.x, grid.c)

    def slab(index, chunk):
        return pl.ds(pl.multiple_of(index * width + chunk * LANES, LANES), LANES)

    loads, load_query, load_last = weight_loads(heads, w_qkv, w_out, w_pair, w_query, w_last, load_sem)
    if not fused:
        for load in loads + [load_query, load_last]:
            load.start()
        grid.greet()

    def ring_copy(way, kind, head, step):
        sign = 1 - 2 * way
        origin = lax.rem(spot_in_ring - sign * (step - 1) + 2 * seq_count, seq_count)
        block = pairs.at[head, origin, kind]
        return remote(block, block, ring_send.at[way, kind, head, step - 1],
                      ring_recv.at[way, kind, head, step - 1], ring_device(spot_in_ring + sign))

    def reach(way, kind):
        return half if way == kind else half - 1

    lines = [(way, kind) for kind in range(2) for way in range(2)]
    for head in range(heads):
        loads[2 * head].wait()
        loads[2 * head + 1].wait()
        made = jnp.dot(normed[...], w_pair[head], preferred_element_type=jnp.float32)
        pairs[head, spot_in_ring, 0] = (rms_scale(made[:, :HDIM]) * key_gain[...]).astype(jnp.bfloat16)
        pairs[head, spot_in_ring, 1] = made[:, HDIM:].astype(jnp.bfloat16)
        for way, kind in lines:
            ring_copy(way, kind, head, 1).start()
    load_query.wait()
    made = jnp.dot(normed[...], w_query[...], preferred_element_type=jnp.float32)
    for head in range(heads):
        one = made[:, head * HDIM:(head + 1) * HDIM]
        queries[head] = (rms_scale(one) * (query_gain[...] / math.sqrt(HDIM))).astype(jnp.bfloat16)
    if not fused:
        fill_chooser(ids, chooser)

    def pass_round(back):
        step = back + 1
        for head in range(heads):
            for way, kind in lines:
                ring_copy(way, kind, head, step).wait_recv()

                if reach(way, kind) == half:
                    ring_copy(way, kind, head, step + 1).start()
                else:
                    @pl.when(step < half - 1)
                    def _():
                        ring_copy(way, kind, head, step + 1).start()

    steps(half - 1, pass_round)
    load_last.wait()
    attended = []
    for head in range(heads):
        for kind in range(2):
            ring_copy(kind, kind, head, half).wait_recv()
        keys = pairs[head, :, 0].reshape(-1, HDIM)
        values = pairs[head, :, 1].reshape(-1, HDIM)
        scores = lax.dot_general(
            queries[head], keys, (((1,), (1,)), ((), ())), preferred_element_type=jnp.float32
        )
        expo = jnp.exp(scores - jnp.max(scores, -1, keepdims=True))
        total = jnp.sum(expo, -1, keepdims=True)
        weighted = jnp.dot(expo.astype(jnp.bfloat16), values, preferred_element_type=jnp.float32)
        attended.append((weighted / total).astype(jnp.bfloat16))
    attended = jnp.concatenate(attended, axis=1)

    spots = [(0, 0, 0)] + grid.chips
    twin_copies = []

    def product(turn, flip):
        y, x, c = grid.shifted(turn, 1)
        if flip:
            c = lax.rem(c + 1, grid.cores)
        start = pl.multiple_of(grid.place(y, x, c) * width, LANES)
        return jnp.dot(attended, w_last[:, pl.ds(start, width)], preferred_element_type=jnp.float32)

    for number, turn in enumerate(spots):
        theirs[number] = product(turn, True)
        copy = remote(theirs.at[number], came.at[number], twin_send.at[number], twin_recv.at[number],
                      grid.sibling())
        copy.start()
        twin_copies.append(copy)
    for number, turn in enumerate(spots):
        mine[number] = product(turn, False)
    for number in range(len(spots)):
        twin_copies[number].wait_recv()
        mine[number] += came[number]
    started, piece_copies = [], []

    def go(copy):
        copy.start()
        started.append(copy)
        return copy

    for chunk in range(chunks):
        copies = []
        for step, turn in enumerate(grid.chips):
            leaving[chunk, step] = mine[step + 1, :, chunk * LANES:(chunk + 1) * LANES].astype(jnp.bfloat16)
            copies.append(go(remote(
                leaving.at[chunk, step], pieces.at[chunk, step], piece_send.at[chunk, step],
                piece_recv.at[chunk, step], grid.to(turn)[1])))
        piece_copies.append(copies)

    def collect(chunk):
        for copy in piece_copies[chunk]:
            copy.wait_recv()
        for ky in range(grid.wide):
            total = mine[0, :, chunk * LANES:(chunk + 1) * LANES] if ky == 0 else None
            for step, turn in enumerate(grid.chips):
                if turn[0] == ky:
                    piece = pieces[chunk, step].astype(jnp.float32)
                    total = piece if total is None else total + piece
            y = lax.rem(grid.y - ky + grid.wide, grid.wide)
            merged[chunk, z, pl.ds(pl.multiple_of(y * merged_rows, merged_rows), merged_rows)] = (
                total * gate[:, slab(me, chunk)]
            ).astype(jnp.bfloat16)

    def upward(chunk, far):
        spot = merged.at[chunk, z - far]
        return remote(spot, spot, up_send.at[chunk, far], up_recv.at[chunk, far], grid.along(z + 1))

    def downward(chunk, far):
        spot = merged.at[chunk, z + far]
        return remote(spot, spot, down_send.at[chunk, far], down_recv.at[chunk, far], grid.along(z - 1))

    def came_up(chunk, far):
        spot = merged.at[chunk, z - far]
        return remote(spot, spot, up_send.at[chunk, far - 1], up_recv.at[chunk, far - 1], grid.along(z + 1))

    def came_down(chunk, far):
        spot = merged.at[chunk, z + far]
        return remote(spot, spot, down_send.at[chunk, far - 1], down_recv.at[chunk, far - 1],
                      grid.along(z - 1))

    def pass_on(chunk, far):
        if far < length - 1:
            @pl.when((z >= far) & (z < length - 1))
            def _():
                upward(chunk, far).start()

            @pl.when((z + far < length) & (z > 0))
            def _():
                downward(chunk, far).start()

    back_copies, keeps = [], []
    for round_number in range(chunks + length - 1):
        for far in range(length):
            chunk = round_number - far
            if not 0 <= chunk < chunks:
                continue
            if far == 0:
                collect(chunk)
            else:
                @pl.when(z >= far)
                def _():
                    came_up(chunk, far).wait_recv()

                @pl.when(z + far < length)
                def _():
                    came_down(chunk, far).wait_recv()
            pass_on(chunk, far)
            if far == length - 1:
                fetched[chunk] = (
                    jnp.dot(
                        chooser[...],
                        merged[chunk].reshape(length * rows, LANES),
                        preferred_element_type=jnp.float32,
                    )
                    .astype(jnp.bfloat16)
                    .reshape(grid.size, src_rows, LANES)
                )
                for step, turn in enumerate(grid.turns):
                    index, device, _ = grid.to(turn)
                    back_copies.append(go(remote(
                        fetched.at[chunk, index], out.at[:, slab(me, chunk)], back_send.at[chunk, step],
                        back_recv.at[chunk, step], device)))
                kept = pltpu.make_async_copy(
                    fetched.at[chunk, me], out.at[:, slab(me, chunk)], keep_sem.at[chunk])
                kept.start()
                keeps.append(kept)
    for head in range(heads):
        for way, kind in lines:
            def sent(back):
                ring_copy(way, kind, head, back + 1).wait_send()

            steps(reach(way, kind), sent)
    for copy in twin_copies:
        copy.wait_send()
    for chunk in range(chunks):
        for far in range(length - 1):
            @pl.when((z >= far) & (z < length - 1))
            def _():
                upward(chunk, far).wait_send()

            @pl.when((z + far < length) & (z > 0))
            def _():
                downward(chunk, far).wait_send()
    for copy in keeps:
        copy.wait()
    for copy in back_copies:
        copy.wait_recv()
    for copy in started:
        copy.wait_send()


def sublayer(tokens, owners, slots, w_qkv, w_out, norm_gain, norm_shift, query_gain, key_gain, out_gate):
    seq_count, head_count = lax.axis_size("seq"), lax.axis_size("head")
    wide = plane_width(seq_count)
    length, size = seq_count // wide, wide * head_count
    src_rows, feature_width = tokens.shape
    width = feature_width // size
    chunks = width // LANES
    merged_rows = src_rows * head_count // RATIO
    rows, labels = wide * merged_rows, size * src_rows
    inner = w_qkv.shape[2]
    heads = inner // HDIM
    cached = length * rows * labels * 4 <= 8 * 2**20
    marks_shape = (length, rows, labels) if cached else (1, 16, LANES)
    dma, turns, spots, half = pltpu.SemaphoreType.DMA, size - 1, size // 2, seq_count // 2
    normed = jax.ShapeDtypeStruct((merged_rows, feature_width), jnp.bfloat16)
    names = jax.ShapeDtypeStruct((size, 1, src_rows), jnp.int32)
    result = jax.ShapeDtypeStruct((src_rows, feature_width), jnp.bfloat16)
    front_scratch = [
        pltpu.VMEM((chunks, size, src_rows, LANES), jnp.bfloat16),
        pltpu.VMEM((chunks, size, src_rows, LANES), jnp.bfloat16),
        pltpu.VMEM((size, 1, src_rows), jnp.int32),
        pltpu.VMEM(marks_shape, jnp.bfloat16),
        pltpu.VMEM(marks_shape, jnp.bfloat16),
        pltpu.VMEM((chunks, length, rows, LANES), jnp.float32),
        pltpu.VMEM((chunks, length + 1, rows, LANES), jnp.float32),
        pltpu.VMEM((chunks, 2, rows, LANES), jnp.float32),
        pltpu.VMEM((size * chunks, merged_rows, LANES), jnp.float32),
        dma((turns,)),
        dma((turns,)),
        dma(()),
        dma(()),
        dma((chunks, turns)),
        dma((chunks, turns)),
        dma((chunks,)),
        dma((chunks, 2)),
        dma((chunks,)),
        dma((chunks, length + 1, wide)),
        dma((chunks, length + 1, wide)),
        dma((chunks, 2, wide)),
        dma((chunks, 2, wide)),
        dma((chunks, spots)),
        dma((chunks, spots)),
        dma((chunks, spots)),
        dma((chunks, spots)),
        pltpu.SemaphoreType.REGULAR,
    ]
    rest_scratch = [
        pltpu.VMEM((heads, feature_width, 2 * HDIM), jnp.bfloat16),
        pltpu.VMEM((feature_width, inner), jnp.bfloat16),
        pltpu.VMEM((inner, feature_width), jnp.bfloat16),
        pltpu.VMEM((heads, seq_count, 2, merged_rows, HDIM), jnp.bfloat16),
        pltpu.VMEM((heads, merged_rows, HDIM), jnp.bfloat16),
        pltpu.VMEM((labels, length * rows), jnp.bfloat16),
        pltpu.VMEM((spots, merged_rows, width), jnp.float32),
        pltpu.VMEM((spots, merged_rows, width), jnp.float32),
        pltpu.VMEM((spots, merged_rows, width), jnp.float32),
        pltpu.VMEM((chunks, spots, merged_rows, LANES), jnp.bfloat16),
        pltpu.VMEM((chunks, spots, merged_rows, LANES), jnp.bfloat16),
        pltpu.VMEM((chunks, length, rows, LANES), jnp.bfloat16),
        pltpu.VMEM((chunks, size, src_rows, LANES), jnp.bfloat16),
        dma((heads + 1, 2)),
        dma((2, 2, heads, half)),
        dma((2, 2, heads, half)),
        dma((spots,)),
        dma((spots,)),
        dma((chunks, spots)),
        dma((chunks, spots)),
        dma((chunks, length)),
        dma((chunks, length)),
        dma((chunks, length)),
        dma((chunks, length)),
        dma((chunks, turns)),
        dma((chunks, turns)),
        dma((chunks,)),
    ]
    front_body = functools.partial(front_kernel, seq_count, head_count, chunks, cached)
    rest_body = functools.partial(rest_kernel, seq_count, head_count, chunks, heads)

    def call(name, number, body, out_shape, in_specs, scratch, arguments):
        return pl.pallas_call(
            body, out_shape=out_shape, in_specs=in_specs,
            out_specs=ANY if out_shape is result else [VMEM] * len(out_shape), scratch_shapes=scratch,
            compiler_params=pltpu.CompilerParams(
                collective_id=number, has_side_effects=True, vmem_limit_bytes=60 * 2**20
            ),
            name=name,
        )(*arguments)

    fused = length * rows * labels <= 2 * 2**20
    if not fused:
        made, ids = call("front", 0, front_body, [normed, names], [ANY] + [VMEM] * 4, front_scratch,
                         (tokens, owners, slots, norm_gain, norm_shift))
        return call("rest", 1, rest_body, result, [VMEM, ANY, ANY] + [VMEM] * 4, rest_scratch,
                    (made, w_qkv, w_out, query_gain, key_gain, out_gate, ids))

    def whole_kernel(*refs):
        front_in, rest_in, out = refs[:5], refs[5:10], refs[10]
        made, ids = refs[11:13]
        front_refs = refs[13:13 + len(front_scratch)]
        rest_refs = refs[13 + len(front_scratch):]
        loads, load_query, load_last = weight_loads(heads, *rest_in[:2], *rest_refs[:3], rest_refs[13])

        def start_loads():
            for load in loads + [load_query, load_last]:
                load.start()

        front_body(*front_in, made, ids, *front_refs, early=start_loads,
                   meanwhile=lambda: fill_chooser(ids, rest_refs[5]))
        rest_body(made, *rest_in, ids, out, *rest_refs, fused=True)

    kept = [pltpu.VMEM(normed.shape, normed.dtype), pltpu.VMEM(names.shape, names.dtype)]
    return call("sublayer", 2, whole_kernel, result, [ANY] + [VMEM] * 4 + [ANY] * 2 + [VMEM] * 3,
                kept + front_scratch + rest_scratch,
                (tokens, owners, slots, norm_gain, norm_shift, w_qkv, w_out, query_gain, key_gain,
                 out_gate))


def on_device(
    tokens,
    owner_shard,
    dest_slot,
    w_qkv,
    w_out,
    norm_gain,
    norm_shift,
    query_gain,
    key_gain,
    out_gate,
):
    return sublayer(tokens, owner_shard.T, dest_slot[None], jnp.transpose(w_qkv, (1, 0, 2)), w_out,
                    norm_gain[None], norm_shift[None], query_gain[None], key_gain[None], out_gate[None])


def solution(mesh):
    placed = (
        P(("seq", "head"), None),
        P(("seq", "head"), None),
        P(("seq", "head")),
        P(None, None, "head"),
        P("head", None),
        P(),
        P(),
        P(),
        P(),
        P(),
    )
    return jax.shard_map(
        on_device, mesh=mesh, in_specs=placed, out_specs=P(("seq", "head"), None), check_vma=False
    )
```

```python
import functools
import math

import jax
import jax.numpy as jnp
from jax import lax
from jax.experimental import pallas as pl
from jax.experimental.pallas import tpu as pltpu
from jax.sharding import PartitionSpec as P

HDIM = 128
RATIO = 4
MESH = pl.DeviceIdType.MESH
ANY = pl.BlockSpec(memory_space=pl.ANY)


def rms_scale(values_in):
    return values_in * lax.rsqrt(jnp.mean(values_in * values_in, -1, keepdims=True) + 1e-06)


def plane_width(seq_count):
    return 2 if seq_count % 2 == 0 else 1


LANES = 128
VMEM = pl.BlockSpec(memory_space=pltpu.VMEM)


def remote(source, target, send, recv, device):
    return pltpu.make_async_remote_copy(
        src_ref=source, dst_ref=target, send_sem=send, recv_sem=recv,
        device_id=device, device_id_type=MESH,
    )


def to_column(row):
    return jnp.transpose(jnp.broadcast_to(row, (LANES, row.shape[1])))[:, :1]


class Grid:
    def __init__(self, seq_count, head_count):
        self.wide = plane_width(seq_count)
        self.heads = head_count
        self.cores = 2 if head_count % 2 == 0 else 1
        self.length = seq_count // self.wide
        self.size = self.wide * head_count
        self.dims = (self.wide, head_count // self.cores, self.cores)
        seq, head = lax.axis_index("seq"), lax.axis_index("head")
        self.z, self.y = seq // self.wide, lax.rem(seq, self.wide)
        self.x, self.c = head // self.cores, lax.rem(head, self.cores)
        self.me = self.place(self.y, self.x, self.c)
        turns = [
            (ky, kx, kc)
            for ky in range(self.dims[0]) for kx in range(self.dims[1]) for kc in range(self.dims[2])
        ]
        self.turns = sorted(turns[1:], key=lambda turn: (turn[0] + turn[1], turn))
        self.chips = [turn for turn in self.turns if turn[2] == 0]

    def place(self, y, x, c):
        return (y * self.dims[1] + x) * self.cores + c

    def shifted(self, turn, sign):
        at = (self.y, self.x, self.c)
        return [lax.rem(at[i] + (sign * turn[i] + self.dims[i]), self.dims[i]) for i in range(3)]

    def to(self, turn):
        y, x, c = self.shifted(turn, 1)
        return self.place(y, x, c), self.device(self.z, y, x, c), y

    def source(self, turn):
        return self.place(*self.shifted(turn, -1))

    def device(self, z, y, x, c):
        return (z * self.wide + y, x * self.cores + c)

    def along(self, z):
        return self.device(z, self.y, self.x, self.c)

    def sibling(self):
        return self.device(self.z, self.y, self.x, lax.rem(self.c + 1, 2))

    def greet(self):
        barrier = pltpu.get_barrier_semaphore()
        last = self.length - 1

        def hail(device):
            pl.semaphore_signal(barrier, inc=1, device_id=device, device_id_type=MESH)

        for turn in self.turns:
            hail(self.to(turn)[1])

        count = len(self.turns)
        for off in (-2, -1, 1, 2):
            there = (self.z + off >= 0) & (self.z + off <= last)
            count = count + jnp.where(there, 1, 0)

            @pl.when(there)
            def _():
                hail(self.along(self.z + off))

        pl.semaphore_wait(barrier, count)


def steps(count, body, reverse=False):
    if count <= 8:
        for number in reversed(range(count)) if reverse else range(count):
            body(number)
    else:
        def one(number, carry):
            body(count - 1 - number if reverse else number)
            return carry
        lax.fori_loop(0, count, one, 0)


def front_kernel(
    seq_count, head_count, chunks, cached, tokens, owners, slots, gain, shift, normed, all_ids, seen,
    far, far_ids, hot, hot_far, part, passing, skip, raw, id_send, id_recv, far_id_send,
    far_id_recv, seen_send, seen_recv, own_sem, far_send, far_recv, pass_send, pass_recv,
    skip_send, skip_recv, raw_send, raw_recv, twin_send, twin_recv, turn_sem,
    early=lambda: None,
):
    grid = Grid(seq_count, head_count)
    z, me, length = grid.z, grid.me, grid.length
    src_rows = tokens.shape[0]
    rows = part.shape[2]
    merged_rows = rows // grid.wide
    width = chunks * LANES
    feature_width = width * grid.size
    low = z < (length + 1) // 2
    sign = jnp.where(low, 1, -1)
    home = jnp.where(low, z, length - 1 - z)
    inward = jnp.where(low, 1, 0)
    outward = 1 - inward
    at_end, near = home == 0, home == 1

    def slab(index, chunk):
        return pl.ds(pl.multiple_of(index * width + chunk * LANES, LANES), LANES)

    all_ids[me] = owners[...] * merged_rows + slots[...]
    grid.greet()
    id_copies, seen_copies, owns = [], [], []
    for step, turn in enumerate(grid.turns):
        copy = remote(all_ids.at[me], all_ids.at[me], id_send.at[step], id_recv.at[step], grid.to(turn)[1])
        copy.start()
        id_copies.append(copy)
    for chunk in range(chunks):
        own = pltpu.make_async_copy(tokens.at[:, slab(me, chunk)], seen.at[chunk, me], own_sem.at[chunk])
        own.start()
        owns.append(own)
        copies = []
        for step, turn in enumerate(grid.turns):
            index, device, _ = grid.to(turn)
            copy = remote(tokens.at[:, slab(index, chunk)], seen.at[chunk, me],
                          seen_send.at[chunk, step], seen_recv.at[chunk, step], device)
            copies.append(copy)
        seen_copies.append(copies)
    for core in range(grid.cores):
        @pl.when(grid.c == core)
        def _():
            for chunk in range(chunks):
                for target in range(grid.cores):
                    for step, turn in enumerate(grid.turns):
                        if (core + turn[2]) % grid.cores == target:
                            seen_copies[chunk][step].start()
    early()

    def far_block(chunk, index, part_number):
        return remote(seen.at[chunk, index], far.at[chunk, index], far_send.at[chunk, part_number],
                      far_recv.at[chunk], grid.along(z + sign))

    def far_half(chunk, part_number):
        blocks = pl.ds(0, grid.size // 2)
        return remote(seen.at[chunk, blocks], far.at[chunk, blocks], far_send.at[chunk, part_number],
                      far_recv.at[chunk], grid.along(z + sign))

    def far_whole(chunk):
        return remote(seen.at[chunk], far.at[chunk], far_send.at[chunk, 0], far_recv.at[chunk],
                      grid.along(z + sign))

    far_names = remote(all_ids, far_ids, far_id_send, far_id_recv, grid.along(z + sign))
    for copy in id_copies:
        copy.wait_recv()

    @pl.when(at_end)
    def _():
        far_names.start()

    places = lax.broadcasted_iota(jnp.int32, (rows, 1), 0)

    def marks(names, dest):
        labels = jnp.concatenate([names[index] for index in range(grid.size)], axis=1)
        return (places + dest * rows == labels).astype(jnp.float32).astype(jnp.bfloat16)

    def summed(chunk, dest):
        chosen = hot[dest] if cached else marks(all_ids, dest)
        return jnp.dot(chosen, seen[chunk].reshape(grid.size * src_rows, LANES),
                       preferred_element_type=jnp.float32)

    def summed_far(chunk, dest):
        chosen = hot_far[dest] if cached else marks(far_ids, dest)
        return jnp.dot(chosen, far[chunk].reshape(grid.size * src_rows, LANES),
                       preferred_element_type=jnp.float32)

    def take_turn(chunk, after):
        if grid.cores == 1:
            return
        if after:
            @pl.when((grid.c == 0) | (chunk < chunks - 1))
            def _():
                pl.semaphore_signal(turn_sem, inc=1, device_id=grid.sibling(), device_id_type=MESH)
        else:
            @pl.when((grid.c == 1) | (chunk > 0))
            def _():
                pl.semaphore_wait(turn_sem, 1)

    @pl.when(at_end)
    def _():
        def begin(chunk):
            owns[chunk].wait()
            far_block(chunk, me, 0).start()

        def follow(chunk, step):
            seen_copies[chunk][step].wait_recv()
            far_block(chunk, grid.source(grid.turns[step]), (step + 1) // (grid.size // 2)).start()

        for chunk in range(chunks):
            take_turn(chunk, 0)
            begin(chunk)
            follow(chunk, 0)
            for step in range(1, len(grid.turns)):
                follow(chunk, step)
            far_half(chunk, 0).wait_send()
            take_turn(chunk, 1)
        if cached:
            hot[z] = marks(all_ids, z)
        for chunk in range(chunks):
            part[chunk, z] = summed(chunk, z)

    @pl.when(jnp.logical_not(at_end))
    def _():
        if cached:
            for dest in range(length):
                hot[dest] = marks(all_ids, dest)

        @pl.when(near)
        def _():
            far_names.wait_recv()
            if cached:
                for dest in range(length):
                    hot_far[dest] = marks(far_ids, dest)

    def block_rows(ky):
        y = lax.rem(grid.y + ky, grid.wide)
        return pl.ds(pl.multiple_of(y * merged_rows, merged_rows), merged_rows)

    order = list(reversed(range(grid.wide)))

    def hop(chunk, dest, direction, sense, ky):
        spot = dest + sense
        return remote(part.at[chunk, dest, block_rows(ky)], passing.at[chunk, spot, block_rows(ky)],
                      pass_send.at[chunk, spot, ky], pass_recv.at[chunk, spot, ky],
                      grid.along(z + direction))

    def leap(chunk, dest, direction, sense, ky):
        return remote(part.at[chunk, dest, block_rows(ky)], skip.at[chunk, sense, block_rows(ky)],
                      skip_send.at[chunk, sense, ky], skip_recv.at[chunk, sense, ky],
                      grid.along(z + 2 * direction))

    def send(chunk, dest, direction, sense, far_off, act):
        for ky in order:
            for kind, here in ((leap, far_off == 2), (hop, far_off != 2)):
                def one():
                    act(kind(chunk, dest, direction, sense, ky))
                if isinstance(far_off, int):
                    if here:
                        one()
                else:
                    pl.when(here)(one)

    def add_passing(chunk, dest, direction, sense):
        for ky in order:
            hop(chunk, dest, direction, sense, ky).wait_recv()
        part[chunk, dest] += passing[chunk, dest + sense]

    def go_now(copy):
        copy.start()

    def away(chunk):
        def one(back):
            far_off = back + 1

            @pl.when(far_off <= length - 1 - home)
            def _():
                dest = z + sign * far_off

                @pl.when(near)
                def _():
                    part[chunk, dest] += summed_far(chunk, dest)

                @pl.when((home >= 2) & (far_off > 1))
                def _():
                    add_passing(chunk, dest, sign, inward)

                send(chunk, dest, sign, inward, far_off, go_now)

        steps(length - 1, one, reverse=True)

        @pl.when(near)
        def _():
            part[chunk, z] += summed_far(chunk, z)

    def home_next(chunk):
        part[chunk, z - sign] = summed(chunk, z - sign)
        send(chunk, z - sign, -sign, outward, 1, go_now)

        def own(far_off):
            @pl.when(far_off <= length - 1 - home)
            def _():
                part[chunk, z + sign * far_off] = summed(chunk, z + sign * far_off)

        steps(length, own)

    def home_far(chunk):
        def one(back):
            far_off = back + 2

            @pl.when(far_off <= home)
            def _():
                dest = z - sign * far_off
                part[chunk, dest] = summed(chunk, dest)
                add_passing(chunk, dest, -sign, outward)
                send(chunk, dest, -sign, outward, far_off, go_now)

        steps(max((length + 1) // 2 - 2, 0), one, reverse=True)

    raw_copies, twin_copies = [], []

    def finish(chunk):
        copies, twins = [None] * len(grid.chips), []
        raw_copies.append(copies)
        twin_copies.append(twins)
        for ky in order:
            where = block_rows(ky)
            sources = [
                (home >= 2, hop, passing, z + inward, sign, inward),
                (home >= 3, leap, skip, inward, sign, inward),
                (home >= 0, hop, passing, z + outward, -sign, outward),
                (home + 2 <= length - 2, leap, skip, outward, -sign, outward),
            ]
            for there, kind, buffer, spot, direction, sense in sources:
                @pl.when(there)
                def _():
                    kind(chunk, z, direction, sense, ky).wait_recv()
                    part[chunk, z, where] += buffer[chunk, spot, where]

            for step, turn in enumerate(grid.chips):
                if turn[0] == ky:
                    copy = remote(part.at[chunk, z, where], raw.at[me * chunks + chunk],
                                  raw_send.at[chunk, step], raw_recv.at[chunk, step], grid.to(turn)[1])
                    copy.start()
                    copies[step] = copy
            if ky == 0:
                raw[me * chunks + chunk] = part[chunk, z, where]
                hand_over(chunk, me, len(grid.chips))

    def hand_over(chunk, index, step):
        if grid.cores == 1:
            return
        spot = raw.at[index * chunks + chunk]
        copy = remote(spot, spot, twin_send.at[chunk, step], twin_recv.at[chunk, step], grid.sibling())
        copy.start()
        twin_copies[chunk].append(copy)

    def pass_over(chunk):
        for step, turn in enumerate(grid.chips):
            raw_copies[chunk][step].wait_recv()
            hand_over(chunk, grid.source(turn), step)

    for chunk in range(chunks):
        @pl.when(jnp.logical_not(at_end))
        def _():
            owns[chunk].wait()
            for copy in seen_copies[chunk]:
                copy.wait_recv()
            home_next(chunk)

            @pl.when(near)
            def _():
                far_whole(chunk).wait_recv()

            away(chunk)

        if chunk > 0:
            finish(chunk - 1)
        if chunk > 1:
            pass_over(chunk - 2)

        @pl.when(jnp.logical_not(at_end))
        def _():
            home_far(chunk)

    finish(chunks - 1)
    for chunk in range(max(chunks - 2, 0), chunks):
        pass_over(chunk)
    for copies in twin_copies:
        for copy in copies:
            copy.wait_recv()
    blocks = grid.size * chunks
    acc = raw[0]
    for block in range(1, blocks):
        acc += raw[block]
    mean = jnp.sum(acc, -1, keepdims=True) * (1.0 / feature_width)
    acc = jnp.zeros_like(acc)
    for block in range(blocks):
        apart = raw[block] - mean
        acc += apart * apart
    scale = lax.rsqrt(jnp.sum(acc, -1, keepdims=True) * (1.0 / feature_width) + 1e-06)
    for block in range(blocks):
        spot = slice(block * LANES, (block + 1) * LANES)
        normed[:, spot] = ((raw[block] - mean) * scale * gain[:, spot] + shift[:, spot]).astype(jnp.bfloat16)

    def done(copy):
        copy.wait_send()

    for copy in id_copies:
        copy.wait_send()
    for chunk in range(chunks):
        for copy in seen_copies[chunk] + raw_copies[chunk] + twin_copies[chunk]:
            copy.wait_send()

    @pl.when(at_end)
    def _():
        far_names.wait_send()
        for chunk in range(chunks):
            far_half(chunk, 1).wait_send()

    @pl.when(jnp.logical_not(at_end))
    def _():
        for chunk in range(chunks):
            def sent(number):
                far_off = number + 1

                @pl.when(far_off <= length - 1 - home)
                def _():
                    send(chunk, z + sign * far_off, sign, inward, far_off, done)

                @pl.when(far_off <= home)
                def _():
                    send(chunk, z - sign * far_off, -sign, outward, far_off, done)

            steps(length - 1, sent)


def weight_loads(heads, w_qkv, w_out, w_pair, w_query, w_last, load_sem):
    loads = []
    for head in range(heads):
        for kind in range(2):
            loads.append(pltpu.make_async_copy(
                w_qkv.at[kind + 1, :, pl.ds(head * HDIM, HDIM)],
                w_pair.at[head, :, pl.ds(kind * HDIM, HDIM)], load_sem.at[head, kind]))
    load_query = pltpu.make_async_copy(w_qkv.at[0], w_query, load_sem.at[heads, 0])
    load_last = pltpu.make_async_copy(w_out, w_last, load_sem.at[heads, 1])
    return loads, load_query, load_last


def fill_chooser(ids, chooser):
    size, src_rows = ids.shape[0], ids.shape[2]
    places = lax.broadcasted_iota(jnp.int32, (1, chooser.shape[1]), 1)
    for index in range(size):
        chooser[index * src_rows:(index + 1) * src_rows] = (
            (to_column(ids[index]) == places).astype(jnp.float32).astype(jnp.bfloat16)
        )


def rest_kernel(
    seq_count, head_count, chunks, heads, normed, w_qkv, w_out, query_gain, key_gain, gate, ids, out,
    w_pair, w_query, w_last, pairs, queries, chooser, theirs, came, mine, leaving, pieces, merged, fetched,
    load_sem, ring_send, ring_recv, twin_send, twin_recv, piece_send, piece_recv, up_send, up_recv,
    down_send, down_recv, back_send, back_recv, keep_sem, fused=False,
):
    grid = Grid(seq_count, head_count)
    z, me, length = grid.z, grid.me, grid.length
    src_rows = out.shape[0]
    merged_rows = normed.shape[0]
    rows = merged.shape[2]
    width = chunks * LANES
    half = seq_count // 2
    spot_in_ring = jnp.where(grid.y == 0, z, seq_count - 1 - z)

    def ring_device(position):
        position = lax.rem(position + seq_count, seq_count)
        low = position < length
        return grid.device(jnp.where(low, position, seq_count - 1 - position),
                           jnp.where(low, 0, 1), grid.x, grid.c)

    def slab(index, chunk):
        return pl.ds(pl.multiple_of(index * width + chunk * LANES, LANES), LANES)

    loads, load_query, load_last = weight_loads(heads, w_qkv, w_out, w_pair, w_query, w_last, load_sem)
    if not fused:
        for load in loads + [load_query, load_last]:
            load.start()
        grid.greet()

    def ring_copy(way, kind, head, step):
        sign = 1 - 2 * way
        origin = lax.rem(spot_in_ring - sign * (step - 1) + 2 * seq_count, seq_count)
        block = pairs.at[head, origin, kind]
        return remote(block, block, ring_send.at[way, kind, head, step - 1],
                      ring_recv.at[way, kind, head, step - 1], ring_device(spot_in_ring + sign))

    def reach(way, kind):
        return half if way == kind else half - 1

    lines = [(way, kind) for kind in range(2) for way in range(2)]
    for head in range(heads):
        loads[2 * head].wait()
        loads[2 * head + 1].wait()
        made = jnp.dot(normed[...], w_pair[head], preferred_element_type=jnp.float32)
        pairs[head, spot_in_ring, 0] = (rms_scale(made[:, :HDIM]) * key_gain[...]).astype(jnp.bfloat16)
        pairs[head, spot_in_ring, 1] = made[:, HDIM:].astype(jnp.bfloat16)
        for way, kind in lines:
            ring_copy(way, kind, head, 1).start()
    def pass_round(back):
        step = back + 1
        for head in range(heads):
            for way, kind in lines:
                ring_copy(way, kind, head, step).wait_recv()

                if reach(way, kind) == half:
                    ring_copy(way, kind, head, step + 1).start()
                else:
                    @pl.when(step < half - 1)
                    def _():
                        ring_copy(way, kind, head, step + 1).start()

    pass_round(0)
    load_query.wait()
    made = jnp.dot(normed[...], w_query[...], preferred_element_type=jnp.float32)
    for head in range(heads):
        one = made[:, head * HDIM:(head + 1) * HDIM]
        queries[head] = (rms_scale(one) * (query_gain[...] / math.sqrt(HDIM))).astype(jnp.bfloat16)
    fill_chooser(ids, chooser)
    steps(half - 2, lambda back: pass_round(back + 1))
    load_last.wait()
    attended = []
    for head in range(heads):
        for kind in range(2):
            ring_copy(kind, kind, head, half).wait_recv()
        keys = pairs[head, :, 0].reshape(-1, HDIM)
        values = pairs[head, :, 1].reshape(-1, HDIM)
        scores = lax.dot_general(
            queries[head], keys, (((1,), (1,)), ((), ())), preferred_element_type=jnp.float32
        )
        expo = jnp.exp(scores - jnp.max(scores, -1, keepdims=True))
        total = jnp.sum(expo, -1, keepdims=True)
        weighted = jnp.dot(expo.astype(jnp.bfloat16), values, preferred_element_type=jnp.float32)
        attended.append((weighted / total).astype(jnp.bfloat16))
    attended = jnp.concatenate(attended, axis=1)

    spots = [(0, 0, 0)] + grid.chips
    def product(turn, flip):
        y, x, c = grid.shifted(turn, 1)
        if flip:
            c = lax.rem(c + 1, grid.cores)
        start = pl.multiple_of(grid.place(y, x, c) * width, LANES)
        return jnp.dot(attended, w_last[:, pl.ds(start, width)], preferred_element_type=jnp.float32)

    backward = list(reversed(list(enumerate(spots))))
    twin_copies = [
        remote(theirs.at[number], came.at[number], twin_send.at[number], twin_recv.at[number],
               grid.sibling())
        for number in range(len(spots))
    ]
    for number, turn in backward:
        theirs[number] = product(turn, True)
        twin_copies[number].start()
    for number, turn in backward:
        mine[number] = product(turn, False)
    started = []

    def go(copy):
        copy.start()
        started.append(copy)
        return copy

    def leave(chunk, number):
        step = number - 1
        leaving[chunk, step] = mine[number, :, chunk * LANES:(chunk + 1) * LANES].astype(jnp.bfloat16)
        return go(remote(
            leaving.at[chunk, step], pieces.at[chunk, step], piece_send.at[chunk, step],
            piece_recv.at[chunk, step], grid.to(spots[number])[1]))

    piece_copies = [[] for _ in range(chunks)]
    for number, turn in backward:
        twin_copies[number].wait_recv()
        mine[number] += came[number]
        if number > 0:
            piece_copies[0].append(leave(0, number))
    for chunk in range(1, chunks):
        for number, turn in backward[:-1]:
            piece_copies[chunk].append(leave(chunk, number))

    def collect(chunk):
        for copy in piece_copies[chunk]:
            copy.wait_recv()
        for ky in range(grid.wide):
            total = mine[0, :, chunk * LANES:(chunk + 1) * LANES] if ky == 0 else None
            for step, turn in enumerate(grid.chips):
                if turn[0] == ky:
                    piece = pieces[chunk, step].astype(jnp.float32)
                    total = piece if total is None else total + piece
            y = lax.rem(grid.y - ky + grid.wide, grid.wide)
            merged[chunk, z, pl.ds(pl.multiple_of(y * merged_rows, merged_rows), merged_rows)] = (
                total * gate[:, slab(me, chunk)]
            ).astype(jnp.bfloat16)

    def upward(chunk, far):
        spot = merged.at[chunk, z - far]
        return remote(spot, spot, up_send.at[chunk, far], up_recv.at[chunk, far], grid.along(z + 1))

    def downward(chunk, far):
        spot = merged.at[chunk, z + far]
        return remote(spot, spot, down_send.at[chunk, far], down_recv.at[chunk, far], grid.along(z - 1))

    def came_up(chunk, far):
        spot = merged.at[chunk, z - far]
        return remote(spot, spot, up_send.at[chunk, far - 1], up_recv.at[chunk, far - 1], grid.along(z + 1))

    def came_down(chunk, far):
        spot = merged.at[chunk, z + far]
        return remote(spot, spot, down_send.at[chunk, far - 1], down_recv.at[chunk, far - 1],
                      grid.along(z - 1))

    def pass_on(chunk, far):
        if far < length - 1:
            @pl.when((z >= far) & (z < length - 1))
            def _():
                upward(chunk, far).start()

            @pl.when((z + far < length) & (z > 0))
            def _():
                downward(chunk, far).start()

    back_copies, keeps = [], []
    for round_number in range(chunks + length - 1):
        for far in range(length):
            chunk = round_number - far
            if not 0 <= chunk < chunks:
                continue
            if far == 0:
                collect(chunk)
            else:
                @pl.when(z >= far)
                def _():
                    came_up(chunk, far).wait_recv()

                @pl.when(z + far < length)
                def _():
                    came_down(chunk, far).wait_recv()
            pass_on(chunk, far)
            if far == length - 1:
                fetched[chunk] = (
                    jnp.dot(
                        chooser[...],
                        merged[chunk].reshape(length * rows, LANES),
                        preferred_element_type=jnp.float32,
                    )
                    .astype(jnp.bfloat16)
                    .reshape(grid.size, src_rows, LANES)
                )
                for step, turn in reversed(list(enumerate(grid.turns))):
                    index, device, _ = grid.to(turn)
                    back_copies.append(go(remote(
                        fetched.at[chunk, index], out.at[:, slab(me, chunk)], back_send.at[chunk, step],
                        back_recv.at[chunk, step], device)))
                kept = pltpu.make_async_copy(
                    fetched.at[chunk, me], out.at[:, slab(me, chunk)], keep_sem.at[chunk])
                kept.start()
                keeps.append(kept)
    for head in range(heads):
        for way, kind in lines:
            def sent(back):
                ring_copy(way, kind, head, back + 1).wait_send()

            steps(reach(way, kind), sent)
    for copy in twin_copies:
        copy.wait_send()
    for chunk in range(chunks):
        for far in range(length - 1):
            @pl.when((z >= far) & (z < length - 1))
            def _():
                upward(chunk, far).wait_send()

            @pl.when((z + far < length) & (z > 0))
            def _():
                downward(chunk, far).wait_send()
    for copy in keeps:
        copy.wait()
    for copy in back_copies:
        copy.wait_recv()
    for copy in started:
        copy.wait_send()


def sublayer(tokens, owners, slots, w_qkv, w_out, norm_gain, norm_shift, query_gain, key_gain, out_gate):
    seq_count, head_count = lax.axis_size("seq"), lax.axis_size("head")
    wide = plane_width(seq_count)
    length, size = seq_count // wide, wide * head_count
    src_rows, feature_width = tokens.shape
    width = feature_width // size
    chunks = width // LANES
    merged_rows = src_rows * head_count // RATIO
    rows, labels = wide * merged_rows, size * src_rows
    inner = w_qkv.shape[2]
    heads = inner // HDIM
    cached = length * rows * labels * 4 <= 8 * 2**20
    marks_shape = (length, rows, labels) if cached else (1, 16, LANES)
    dma, turns, spots, half = pltpu.SemaphoreType.DMA, size - 1, size // 2, seq_count // 2
    normed = jax.ShapeDtypeStruct((merged_rows, feature_width), jnp.bfloat16)
    names = jax.ShapeDtypeStruct((size, 1, src_rows), jnp.int32)
    result = jax.ShapeDtypeStruct((src_rows, feature_width), jnp.bfloat16)
    front_scratch = [
        pltpu.VMEM((chunks, size, src_rows, LANES), jnp.bfloat16),
        pltpu.VMEM((chunks, size, src_rows, LANES), jnp.bfloat16),
        pltpu.VMEM((size, 1, src_rows), jnp.int32),
        pltpu.VMEM(marks_shape, jnp.bfloat16),
        pltpu.VMEM(marks_shape, jnp.bfloat16),
        pltpu.VMEM((chunks, length, rows, LANES), jnp.float32),
        pltpu.VMEM((chunks, length + 1, rows, LANES), jnp.float32),
        pltpu.VMEM((chunks, 2, rows, LANES), jnp.float32),
        pltpu.VMEM((size * chunks, merged_rows, LANES), jnp.float32),
        dma((turns,)),
        dma((turns,)),
        dma(()),
        dma(()),
        dma((chunks, turns)),
        dma((chunks, turns)),
        dma((chunks,)),
        dma((chunks, 2)),
        dma((chunks,)),
        dma((chunks, length + 1, wide)),
        dma((chunks, length + 1, wide)),
        dma((chunks, 2, wide)),
        dma((chunks, 2, wide)),
        dma((chunks, spots)),
        dma((chunks, spots)),
        dma((chunks, spots)),
        dma((chunks, spots)),
        pltpu.SemaphoreType.REGULAR,
    ]
    rest_scratch = [
        pltpu.VMEM((heads, feature_width, 2 * HDIM), jnp.bfloat16),
        pltpu.VMEM((feature_width, inner), jnp.bfloat16),
        pltpu.VMEM((inner, feature_width), jnp.bfloat16),
        pltpu.VMEM((heads, seq_count, 2, merged_rows, HDIM), jnp.bfloat16),
        pltpu.VMEM((heads, merged_rows, HDIM), jnp.bfloat16),
        pltpu.VMEM((labels, length * rows), jnp.bfloat16),
        pltpu.VMEM((spots, merged_rows, width), jnp.float32),
        pltpu.VMEM((spots, merged_rows, width), jnp.float32),
        pltpu.VMEM((spots, merged_rows, width), jnp.float32),
        pltpu.VMEM((chunks, spots, merged_rows, LANES), jnp.bfloat16),
        pltpu.VMEM((chunks, spots, merged_rows, LANES), jnp.bfloat16),
        pltpu.VMEM((chunks, length, rows, LANES), jnp.bfloat16),
        pltpu.VMEM((chunks, size, src_rows, LANES), jnp.bfloat16),
        dma((heads + 1, 2)),
        dma((2, 2, heads, half)),
        dma((2, 2, heads, half)),
        dma((spots,)),
        dma((spots,)),
        dma((chunks, spots)),
        dma((chunks, spots)),
        dma((chunks, length)),
        dma((chunks, length)),
        dma((chunks, length)),
        dma((chunks, length)),
        dma((chunks, turns)),
        dma((chunks, turns)),
        dma((chunks,)),
    ]
    front_body = functools.partial(front_kernel, seq_count, head_count, chunks, cached)
    rest_body = functools.partial(rest_kernel, seq_count, head_count, chunks, heads)

    def call(name, number, body, out_shape, in_specs, scratch, arguments):
        return pl.pallas_call(
            body, out_shape=out_shape, in_specs=in_specs,
            out_specs=ANY if out_shape is result else [VMEM] * len(out_shape), scratch_shapes=scratch,
            compiler_params=pltpu.CompilerParams(
                collective_id=number, has_side_effects=True, vmem_limit_bytes=60 * 2**20
            ),
            name=name,
        )(*arguments)

    fused = length * rows * labels <= 2 * 2**20
    if not fused:
        made, ids = call("front", 0, front_body, [normed, names], [ANY] + [VMEM] * 4, front_scratch,
                         (tokens, owners, slots, norm_gain, norm_shift))
        return call("rest", 1, rest_body, result, [VMEM, ANY, ANY] + [VMEM] * 4, rest_scratch,
                    (made, w_qkv, w_out, query_gain, key_gain, out_gate, ids))

    def whole_kernel(*refs):
        front_in, rest_in, out = refs[:5], refs[5:10], refs[10]
        made, ids = refs[11:13]
        front_refs = refs[13:13 + len(front_scratch)]
        rest_refs = refs[13 + len(front_scratch):]
        loads, load_query, load_last = weight_loads(heads, *rest_in[:2], *rest_refs[:3], rest_refs[13])

        def start_loads():
            for load in loads + [load_query, load_last]:
                load.start()

        front_body(*front_in, made, ids, *front_refs, early=start_loads)
        rest_body(made, *rest_in, ids, out, *rest_refs, fused=True)

    kept = [pltpu.VMEM(normed.shape, normed.dtype), pltpu.VMEM(names.shape, names.dtype)]
    return call("sublayer", 2, whole_kernel, result, [ANY] + [VMEM] * 4 + [ANY] * 2 + [VMEM] * 3,
                kept + front_scratch + rest_scratch,
                (tokens, owners, slots, norm_gain, norm_shift, w_qkv, w_out, query_gain, key_gain,
                 out_gate))


def on_device(
    tokens,
    owner_shard,
    dest_slot,
    w_qkv,
    w_out,
    norm_gain,
    norm_shift,
    query_gain,
    key_gain,
    out_gate,
):
    return sublayer(tokens, owner_shard.T, dest_slot[None], jnp.transpose(w_qkv, (1, 0, 2)), w_out,
                    norm_gain[None], norm_shift[None], query_gain[None], key_gain[None], out_gate[None])


def solution(mesh):
    placed = (
        P(("seq", "head"), None),
        P(("seq", "head"), None),
        P(("seq", "head")),
        P(None, None, "head"),
        P("head", None),
        P(),
        P(),
        P(),
        P(),
        P(),
    )
    return jax.shard_map(
        on_device, mesh=mesh, in_specs=placed, out_specs=P(("seq", "head"), None), check_vma=False
    )
```

```python
import functools
import math

import jax
import jax.numpy as jnp
from jax import lax
from jax.experimental import pallas as pl
from jax.experimental.pallas import tpu as pltpu
from jax.sharding import PartitionSpec as P

HDIM = 128
RATIO = 4
MESH = pl.DeviceIdType.MESH
ANY = pl.BlockSpec(memory_space=pl.ANY)


def rms_scale(values_in):
    return values_in * lax.rsqrt(jnp.mean(values_in * values_in, -1, keepdims=True) + 1e-06)


def plane_width(seq_count):
    return 2 if seq_count % 2 == 0 else 1


LANES = 128
VMEM = pl.BlockSpec(memory_space=pltpu.VMEM)


def remote(source, target, send, recv, device):
    return pltpu.make_async_remote_copy(
        src_ref=source, dst_ref=target, send_sem=send, recv_sem=recv,
        device_id=device, device_id_type=MESH,
    )


def to_column(row):
    return jnp.transpose(jnp.broadcast_to(row, (LANES, row.shape[1])))[:, :1]


class Grid:
    def __init__(self, seq_count, head_count):
        self.wide = plane_width(seq_count)
        self.heads = head_count
        self.cores = 2 if head_count % 2 == 0 else 1
        self.length = seq_count // self.wide
        self.size = self.wide * head_count
        self.dims = (self.wide, head_count // self.cores, self.cores)
        seq, head = lax.axis_index("seq"), lax.axis_index("head")
        self.z, self.y = seq // self.wide, lax.rem(seq, self.wide)
        self.x, self.c = head // self.cores, lax.rem(head, self.cores)
        self.me = self.place(self.y, self.x, self.c)
        turns = [
            (ky, kx, kc)
            for ky in range(self.dims[0]) for kx in range(self.dims[1]) for kc in range(self.dims[2])
        ]
        self.turns = sorted(turns[1:], key=lambda turn: (turn[0] + turn[1], turn))
        self.chips = [turn for turn in self.turns if turn[2] == 0]

    def place(self, y, x, c):
        return (y * self.dims[1] + x) * self.cores + c

    def shifted(self, turn, sign):
        at = (self.y, self.x, self.c)
        return [lax.rem(at[i] + (sign * turn[i] + self.dims[i]), self.dims[i]) for i in range(3)]

    def to(self, turn):
        y, x, c = self.shifted(turn, 1)
        return self.place(y, x, c), self.device(self.z, y, x, c), y

    def source(self, turn):
        return self.place(*self.shifted(turn, -1))

    def device(self, z, y, x, c):
        return (z * self.wide + y, x * self.cores + c)

    def along(self, z):
        return self.device(z, self.y, self.x, self.c)

    def sibling(self):
        return self.device(self.z, self.y, self.x, lax.rem(self.c + 1, 2))

    def greet(self):
        barrier = pltpu.get_barrier_semaphore()
        last = self.length - 1

        def hail(device):
            pl.semaphore_signal(barrier, inc=1, device_id=device, device_id_type=MESH)

        for turn in self.turns:
            hail(self.to(turn)[1])

        count = len(self.turns)
        for off in (-2, -1, 1, 2):
            there = (self.z + off >= 0) & (self.z + off <= last)
            count = count + jnp.where(there, 1, 0)

            @pl.when(there)
            def _():
                hail(self.along(self.z + off))

        pl.semaphore_wait(barrier, count)


def steps(count, body, reverse=False):
    if count <= 8:
        for number in reversed(range(count)) if reverse else range(count):
            body(number)
    else:
        def one(number, carry):
            body(count - 1 - number if reverse else number)
            return carry
        lax.fori_loop(0, count, one, 0)


def front_kernel(
    seq_count, head_count, chunks, cached, tokens, owners, slots, gain, shift, normed, all_ids, seen,
    far, far_ids, hot, hot_far, part, passing, skip, raw, id_send, id_recv, far_id_send,
    far_id_recv, seen_send, seen_recv, own_sem, far_send, far_recv, pass_send, pass_recv,
    skip_send, skip_recv, raw_send, raw_recv, twin_send, twin_recv, turn_sem,
    early=lambda: None,
):
    grid = Grid(seq_count, head_count)
    z, me, length = grid.z, grid.me, grid.length
    src_rows = tokens.shape[0]
    rows = part.shape[2]
    merged_rows = rows // grid.wide
    width = chunks * LANES
    feature_width = width * grid.size
    low = z < (length + 1) // 2
    sign = jnp.where(low, 1, -1)
    home = jnp.where(low, z, length - 1 - z)
    inward = jnp.where(low, 1, 0)
    outward = 1 - inward
    at_end, near = home == 0, home == 1

    def slab(index, chunk):
        return pl.ds(pl.multiple_of(index * width + chunk * LANES, LANES), LANES)

    all_ids[me] = owners[...] * merged_rows + slots[...]
    grid.greet()
    id_copies, seen_copies, owns = [], [], []
    for step, turn in enumerate(grid.turns):
        copy = remote(all_ids.at[me], all_ids.at[me], id_send.at[step], id_recv.at[step], grid.to(turn)[1])
        copy.start()
        id_copies.append(copy)
    for chunk in range(chunks):
        own = pltpu.make_async_copy(tokens.at[:, slab(me, chunk)], seen.at[chunk, me], own_sem.at[chunk])
        own.start()
        owns.append(own)
        copies = []
        for step, turn in enumerate(grid.turns):
            index, device, _ = grid.to(turn)
            copy = remote(tokens.at[:, slab(index, chunk)], seen.at[chunk, me],
                          seen_send.at[chunk, step], seen_recv.at[chunk, step], device)
            copies.append(copy)
        seen_copies.append(copies)
    for core in range(grid.cores):
        @pl.when(grid.c == core)
        def _():
            for chunk in range(chunks):
                for target in range(grid.cores):
                    for step, turn in enumerate(grid.turns):
                        if (core + turn[2]) % grid.cores == target:
                            seen_copies[chunk][step].start()
    early()

    def far_block(chunk, index, part_number):
        return remote(seen.at[chunk, index], far.at[chunk, index], far_send.at[chunk, part_number],
                      far_recv.at[chunk], grid.along(z + sign))

    def far_half(chunk, part_number):
        blocks = pl.ds(0, grid.size // 2)
        return remote(seen.at[chunk, blocks], far.at[chunk, blocks], far_send.at[chunk, part_number],
                      far_recv.at[chunk], grid.along(z + sign))

    def far_whole(chunk):
        return remote(seen.at[chunk], far.at[chunk], far_send.at[chunk, 0], far_recv.at[chunk],
                      grid.along(z + sign))

    far_names = remote(all_ids, far_ids, far_id_send, far_id_recv, grid.along(z + sign))
    for copy in id_copies:
        copy.wait_recv()

    @pl.when(at_end)
    def _():
        far_names.start()

    places = lax.broadcasted_iota(jnp.int32, (rows, 1), 0)

    def marks(names, dest):
        labels = jnp.concatenate([names[index] for index in range(grid.size)], axis=1)
        return (places + dest * rows == labels).astype(jnp.float32).astype(jnp.bfloat16)

    def summed(chunk, dest):
        chosen = hot[dest] if cached else marks(all_ids, dest)
        return jnp.dot(chosen, seen[chunk].reshape(grid.size * src_rows, LANES),
                       preferred_element_type=jnp.float32)

    def summed_far(chunk, dest):
        chosen = hot_far[dest] if cached else marks(far_ids, dest)
        return jnp.dot(chosen, far[chunk].reshape(grid.size * src_rows, LANES),
                       preferred_element_type=jnp.float32)

    def take_turn(chunk, after):
        if grid.cores == 1:
            return
        if after:
            @pl.when((grid.c == 0) | (chunk < chunks - 1))
            def _():
                pl.semaphore_signal(turn_sem, inc=1, device_id=grid.sibling(), device_id_type=MESH)
        else:
            @pl.when((grid.c == 1) | (chunk > 0))
            def _():
                pl.semaphore_wait(turn_sem, 1)

    @pl.when(at_end)
    def _():
        def begin(chunk):
            owns[chunk].wait()
            far_block(chunk, me, 0).start()

        def follow(chunk, step):
            seen_copies[chunk][step].wait_recv()
            far_block(chunk, grid.source(grid.turns[step]), (step + 1) // (grid.size // 2)).start()

        for chunk in range(chunks):
            take_turn(chunk, 0)
            begin(chunk)
            follow(chunk, 0)
            for step in range(1, len(grid.turns)):
                follow(chunk, step)
            far_half(chunk, 0).wait_send()
            take_turn(chunk, 1)
        if cached:
            hot[z] = marks(all_ids, z)
        for chunk in range(chunks):
            part[chunk, z] = summed(chunk, z)

    @pl.when(jnp.logical_not(at_end))
    def _():
        if cached:
            for dest in range(length):
                hot[dest] = marks(all_ids, dest)

        @pl.when(near)
        def _():
            far_names.wait_recv()
            if cached:
                for dest in range(length):
                    hot_far[dest] = marks(far_ids, dest)

    def block_rows(ky):
        y = lax.rem(grid.y + ky, grid.wide)
        return pl.ds(pl.multiple_of(y * merged_rows, merged_rows), merged_rows)

    order = list(reversed(range(grid.wide)))

    def hop(chunk, dest, direction, sense, ky):
        spot = dest + sense
        return remote(part.at[chunk, dest, block_rows(ky)], passing.at[chunk, spot, block_rows(ky)],
                      pass_send.at[chunk, spot, ky], pass_recv.at[chunk, spot, ky],
                      grid.along(z + direction))

    def leap(chunk, dest, direction, sense, ky):
        return remote(part.at[chunk, dest, block_rows(ky)], skip.at[chunk, sense, block_rows(ky)],
                      skip_send.at[chunk, sense, ky], skip_recv.at[chunk, sense, ky],
                      grid.along(z + 2 * direction))

    def send(chunk, dest, direction, sense, far_off, act):
        for ky in order:
            for kind, here in ((leap, far_off == 2), (hop, far_off != 2)):
                def one():
                    act(kind(chunk, dest, direction, sense, ky))
                if isinstance(far_off, int):
                    if here:
                        one()
                else:
                    pl.when(here)(one)

    def add_passing(chunk, dest, direction, sense):
        for ky in order:
            hop(chunk, dest, direction, sense, ky).wait_recv()
        part[chunk, dest] += passing[chunk, dest + sense]

    def go_now(copy):
        copy.start()

    def away(chunk):
        def one(back):
            far_off = back + 1

            @pl.when(far_off <= length - 1 - home)
            def _():
                dest = z + sign * far_off

                @pl.when(near)
                def _():
                    part[chunk, dest] += summed_far(chunk, dest)

                @pl.when((home >= 2) & (far_off > 1))
                def _():
                    add_passing(chunk, dest, sign, inward)

                send(chunk, dest, sign, inward, far_off, go_now)

        steps(length - 1, one, reverse=True)

        @pl.when(near)
        def _():
            part[chunk, z] += summed_far(chunk, z)

    def home_next(chunk):
        part[chunk, z - sign] = summed(chunk, z - sign)
        send(chunk, z - sign, -sign, outward, 1, go_now)

        def own(far_off):
            @pl.when(far_off <= length - 1 - home)
            def _():
                part[chunk, z + sign * far_off] = summed(chunk, z + sign * far_off)

        steps(length, own)

    def home_far(chunk):
        def one(back):
            far_off = back + 2

            @pl.when(far_off <= home)
            def _():
                dest = z - sign * far_off
                part[chunk, dest] = summed(chunk, dest)
                add_passing(chunk, dest, -sign, outward)
                send(chunk, dest, -sign, outward, far_off, go_now)

        steps(max((length + 1) // 2 - 2, 0), one, reverse=True)

    raw_copies, twin_copies = [], []

    def finish(chunk):
        copies, twins = [None] * len(grid.chips), []
        raw_copies.append(copies)
        twin_copies.append(twins)
        for ky in order:
            where = block_rows(ky)
            sources = [
                (home >= 2, hop, passing, z + inward, sign, inward),
                (home >= 3, leap, skip, inward, sign, inward),
                (home >= 0, hop, passing, z + outward, -sign, outward),
                (home + 2 <= length - 2, leap, skip, outward, -sign, outward),
            ]
            for there, kind, buffer, spot, direction, sense in sources:
                @pl.when(there)
                def _():
                    kind(chunk, z, direction, sense, ky).wait_recv()
                    part[chunk, z, where] += buffer[chunk, spot, where]

            for step, turn in enumerate(grid.chips):
                if turn[0] == ky:
                    copy = remote(part.at[chunk, z, where], raw.at[me * chunks + chunk],
                                  raw_send.at[chunk, step], raw_recv.at[chunk, step], grid.to(turn)[1])
                    copy.start()
                    copies[step] = copy
            if ky == 0:
                raw[me * chunks + chunk] = part[chunk, z, where]
                hand_over(chunk, me, len(grid.chips))

    def hand_over(chunk, index, step):
        if grid.cores == 1:
            return
        spot = raw.at[index * chunks + chunk]
        copy = remote(spot, spot, twin_send.at[chunk, step], twin_recv.at[chunk, step], grid.sibling())
        copy.start()
        twin_copies[chunk].append(copy)

    def pass_over(chunk):
        for step, turn in enumerate(grid.chips):
            raw_copies[chunk][step].wait_recv()
            hand_over(chunk, grid.source(turn), step)

    for chunk in range(chunks):
        @pl.when(jnp.logical_not(at_end))
        def _():
            owns[chunk].wait()
            for copy in seen_copies[chunk]:
                copy.wait_recv()
            home_next(chunk)

            @pl.when(near)
            def _():
                far_whole(chunk).wait_recv()

            away(chunk)

        if chunk > 0:
            finish(chunk - 1)
        if chunk > 1:
            pass_over(chunk - 2)

        @pl.when(jnp.logical_not(at_end))
        def _():
            home_far(chunk)

    finish(chunks - 1)
    for chunk in range(max(chunks - 2, 0), chunks):
        pass_over(chunk)
    for copies in twin_copies:
        for copy in copies:
            copy.wait_recv()
    blocks = grid.size * chunks
    acc = raw[0]
    for block in range(1, blocks):
        acc += raw[block]
    mean = jnp.sum(acc, -1, keepdims=True) * (1.0 / feature_width)
    acc = jnp.zeros_like(acc)
    for block in range(blocks):
        apart = raw[block] - mean
        acc += apart * apart
    scale = lax.rsqrt(jnp.sum(acc, -1, keepdims=True) * (1.0 / feature_width) + 1e-06)
    for block in range(blocks):
        spot = slice(block * LANES, (block + 1) * LANES)
        normed[:, spot] = ((raw[block] - mean) * scale * gain[:, spot] + shift[:, spot]).astype(jnp.bfloat16)

    def done(copy):
        copy.wait_send()

    for copy in id_copies:
        copy.wait_send()
    for chunk in range(chunks):
        for copy in seen_copies[chunk] + raw_copies[chunk] + twin_copies[chunk]:
            copy.wait_send()

    @pl.when(at_end)
    def _():
        far_names.wait_send()
        for chunk in range(chunks):
            far_half(chunk, 1).wait_send()

    @pl.when(jnp.logical_not(at_end))
    def _():
        for chunk in range(chunks):
            def sent(number):
                far_off = number + 1

                @pl.when(far_off <= length - 1 - home)
                def _():
                    send(chunk, z + sign * far_off, sign, inward, far_off, done)

                @pl.when(far_off <= home)
                def _():
                    send(chunk, z - sign * far_off, -sign, outward, far_off, done)

            steps(length - 1, sent)


def weight_loads(heads, w_qkv, w_out, w_pair, w_query, w_last, load_sem):
    loads = []
    for head in range(heads):
        for kind in range(2):
            loads.append(pltpu.make_async_copy(
                w_qkv.at[kind + 1, :, pl.ds(head * HDIM, HDIM)],
                w_pair.at[head, :, pl.ds(kind * HDIM, HDIM)], load_sem.at[head, kind]))
    load_query = pltpu.make_async_copy(w_qkv.at[0], w_query, load_sem.at[heads, 0])
    load_last = pltpu.make_async_copy(w_out, w_last, load_sem.at[heads, 1])
    return loads, load_query, load_last


def fill_chooser(ids, chooser):
    size, src_rows = ids.shape[0], ids.shape[2]
    places = lax.broadcasted_iota(jnp.int32, (1, chooser.shape[1]), 1)
    for index in range(size):
        chooser[index * src_rows:(index + 1) * src_rows] = (
            (to_column(ids[index]) == places).astype(jnp.float32).astype(jnp.bfloat16)
        )


def rest_kernel(
    seq_count, head_count, chunks, heads, normed, w_qkv, w_out, query_gain, key_gain, gate, ids, out,
    w_pair, w_query, w_last, pairs, queries, chooser, theirs, came, mine, leaving, pieces, merged, fetched,
    load_sem, ring_send, ring_recv, twin_send, twin_recv, piece_send, piece_recv, up_send, up_recv,
    down_send, down_recv, back_send, back_recv, keep_sem, fused=False,
):
    grid = Grid(seq_count, head_count)
    z, me, length = grid.z, grid.me, grid.length
    src_rows = out.shape[0]
    merged_rows = normed.shape[0]
    rows = merged.shape[2]
    width = chunks * LANES
    half = seq_count // 2
    spot_in_ring = jnp.where(grid.y == 0, z, seq_count - 1 - z)

    def ring_device(position):
        position = lax.rem(position + seq_count, seq_count)
        low = position < length
        return grid.device(jnp.where(low, position, seq_count - 1 - position),
                           jnp.where(low, 0, 1), grid.x, grid.c)

    def slab(index, chunk):
        return pl.ds(pl.multiple_of(index * width + chunk * LANES, LANES), LANES)

    loads, load_query, load_last = weight_loads(heads, w_qkv, w_out, w_pair, w_query, w_last, load_sem)
    if not fused:
        for load in loads + [load_query, load_last]:
            load.start()
        grid.greet()

    def ring_copy(way, kind, head, step):
        sign = 1 - 2 * way
        origin = lax.rem(spot_in_ring - sign * (step - 1) + 2 * seq_count, seq_count)
        block = pairs.at[head, origin, kind]
        return remote(block, block, ring_send.at[way, kind, head, step - 1],
                      ring_recv.at[way, kind, head, step - 1], ring_device(spot_in_ring + sign))

    def ring_both(way, head, step):
        sign = 1 - 2 * way
        origin = lax.rem(spot_in_ring - sign * (step - 1) + 2 * seq_count, seq_count)
        block = pairs.at[head, origin]
        return remote(block, block, ring_send.at[way, 0, head, step - 1],
                      ring_recv.at[way, 0, head, step - 1], ring_device(spot_in_ring + sign))

    for head in range(heads):
        loads[2 * head].wait()
        loads[2 * head + 1].wait()
        made = jnp.dot(normed[...], w_pair[head], preferred_element_type=jnp.float32)
        pairs[head, spot_in_ring, 0] = (rms_scale(made[:, :HDIM]) * key_gain[...]).astype(jnp.bfloat16)
        pairs[head, spot_in_ring, 1] = made[:, HDIM:].astype(jnp.bfloat16)
        for way in range(2):
            ring_both(way, head, 1).start()
    def pass_round(back):
        step = back + 1
        for head in range(heads):
            for way in range(2):
                ring_both(way, head, step).wait_recv()

                @pl.when(step < half - 1)
                def _():
                    ring_both(way, head, step + 1).start()

                @pl.when(step == half - 1)
                def _():
                    ring_copy(way, way, head, half).start()

    pass_round(0)
    load_query.wait()
    made = jnp.dot(normed[...], w_query[...], preferred_element_type=jnp.float32)
    for head in range(heads):
        one = made[:, head * HDIM:(head + 1) * HDIM]
        queries[head] = (rms_scale(one) * (query_gain[...] / math.sqrt(HDIM))).astype(jnp.bfloat16)
    fill_chooser(ids, chooser)
    steps(half - 2, lambda back: pass_round(back + 1))
    load_last.wait()
    attended = []
    for head in range(heads):
        for kind in range(2):
            ring_copy(kind, kind, head, half).wait_recv()
        keys = pairs[head, :, 0].reshape(-1, HDIM)
        values = pairs[head, :, 1].reshape(-1, HDIM)
        scores = lax.dot_general(
            queries[head], keys, (((1,), (1,)), ((), ())), preferred_element_type=jnp.float32
        )
        expo = jnp.exp(scores - jnp.max(scores, -1, keepdims=True))
        total = jnp.sum(expo, -1, keepdims=True)
        weighted = jnp.dot(expo.astype(jnp.bfloat16), values, preferred_element_type=jnp.float32)
        attended.append((weighted / total).astype(jnp.bfloat16))
    attended = jnp.concatenate(attended, axis=1)

    spots = [(0, 0, 0)] + grid.chips
    def product(turn, flip):
        y, x, c = grid.shifted(turn, 1)
        if flip:
            c = lax.rem(c + 1, grid.cores)
        start = pl.multiple_of(grid.place(y, x, c) * width, LANES)
        return jnp.dot(attended, w_last[:, pl.ds(start, width)], preferred_element_type=jnp.float32)

    backward = list(reversed(list(enumerate(spots))))
    twin_copies = [
        remote(theirs.at[number], came.at[number], twin_send.at[number], twin_recv.at[number],
               grid.sibling())
        for number in range(len(spots))
    ]
    for number, turn in backward:
        theirs[number] = product(turn, True)
        twin_copies[number].start()
    for number, turn in backward:
        mine[number] = product(turn, False)
    started = []

    def go(copy):
        copy.start()
        started.append(copy)
        return copy

    def leave(chunk, number):
        step = number - 1
        leaving[chunk, step] = mine[number, :, chunk * LANES:(chunk + 1) * LANES].astype(jnp.bfloat16)
        return go(remote(
            leaving.at[chunk, step], pieces.at[chunk, step], piece_send.at[chunk, step],
            piece_recv.at[chunk, step], grid.to(spots[number])[1]))

    piece_copies = [[] for _ in range(chunks)]
    for number, turn in backward:
        twin_copies[number].wait_recv()
        mine[number] += came[number]
        if number > 0:
            piece_copies[0].append(leave(0, number))
    for chunk in range(1, chunks):
        for number, turn in backward[:-1]:
            piece_copies[chunk].append(leave(chunk, number))

    def collect(chunk):
        for copy in piece_copies[chunk]:
            copy.wait_recv()
        for ky in range(grid.wide):
            total = mine[0, :, chunk * LANES:(chunk + 1) * LANES] if ky == 0 else None
            for step, turn in enumerate(grid.chips):
                if turn[0] == ky:
                    piece = pieces[chunk, step].astype(jnp.float32)
                    total = piece if total is None else total + piece
            y = lax.rem(grid.y - ky + grid.wide, grid.wide)
            merged[chunk, z, pl.ds(pl.multiple_of(y * merged_rows, merged_rows), merged_rows)] = (
                total * gate[:, slab(me, chunk)]
            ).astype(jnp.bfloat16)

    def upward(chunk, far):
        spot = merged.at[chunk, z - far]
        return remote(spot, spot, up_send.at[chunk, far], up_recv.at[chunk, far], grid.along(z + 1))

    def downward(chunk, far):
        spot = merged.at[chunk, z + far]
        return remote(spot, spot, down_send.at[chunk, far], down_recv.at[chunk, far], grid.along(z - 1))

    def came_up(chunk, far):
        spot = merged.at[chunk, z - far]
        return remote(spot, spot, up_send.at[chunk, far - 1], up_recv.at[chunk, far - 1], grid.along(z + 1))

    def came_down(chunk, far):
        spot = merged.at[chunk, z + far]
        return remote(spot, spot, down_send.at[chunk, far - 1], down_recv.at[chunk, far - 1],
                      grid.along(z - 1))

    def pass_on(chunk, far):
        if far < length - 1:
            @pl.when((z >= far) & (z < length - 1))
            def _():
                upward(chunk, far).start()

            @pl.when((z + far < length) & (z > 0))
            def _():
                downward(chunk, far).start()

    back_copies, keeps = [], []
    for round_number in range(chunks + length - 1):
        for far in range(length):
            chunk = round_number - far
            if not 0 <= chunk < chunks:
                continue
            if far == 0:
                collect(chunk)
            else:
                @pl.when(z >= far)
                def _():
                    came_up(chunk, far).wait_recv()

                @pl.when(z + far < length)
                def _():
                    came_down(chunk, far).wait_recv()
            pass_on(chunk, far)
            if far == length - 1:
                fetched[chunk] = (
                    jnp.dot(
                        chooser[...],
                        merged[chunk].reshape(length * rows, LANES),
                        preferred_element_type=jnp.float32,
                    )
                    .astype(jnp.bfloat16)
                    .reshape(grid.size, src_rows, LANES)
                )
                for step, turn in reversed(list(enumerate(grid.turns))):
                    index, device, _ = grid.to(turn)
                    back_copies.append(go(remote(
                        fetched.at[chunk, index], out.at[:, slab(me, chunk)], back_send.at[chunk, step],
                        back_recv.at[chunk, step], device)))
                kept = pltpu.make_async_copy(
                    fetched.at[chunk, me], out.at[:, slab(me, chunk)], keep_sem.at[chunk])
                kept.start()
                keeps.append(kept)
    for head in range(heads):
        for way in range(2):
            def sent(back):
                ring_both(way, head, back + 1).wait_send()

            steps(half - 1, sent)
            ring_copy(way, way, head, half).wait_send()
    for copy in twin_copies:
        copy.wait_send()
    for chunk in range(chunks):
        for far in range(length - 1):
            @pl.when((z >= far) & (z < length - 1))
            def _():
                upward(chunk, far).wait_send()

            @pl.when((z + far < length) & (z > 0))
            def _():
                downward(chunk, far).wait_send()
    for copy in keeps:
        copy.wait()
    for copy in back_copies:
        copy.wait_recv()
    for copy in started:
        copy.wait_send()


def sublayer(tokens, owners, slots, w_qkv, w_out, norm_gain, norm_shift, query_gain, key_gain, out_gate):
    seq_count, head_count = lax.axis_size("seq"), lax.axis_size("head")
    wide = plane_width(seq_count)
    length, size = seq_count // wide, wide * head_count
    src_rows, feature_width = tokens.shape
    width = feature_width // size
    chunks = width // LANES
    merged_rows = src_rows * head_count // RATIO
    rows, labels = wide * merged_rows, size * src_rows
    inner = w_qkv.shape[2]
    heads = inner // HDIM
    cached = length * rows * labels * 4 <= 8 * 2**20
    marks_shape = (length, rows, labels) if cached else (1, 16, LANES)
    dma, turns, spots, half = pltpu.SemaphoreType.DMA, size - 1, size // 2, seq_count // 2
    normed = jax.ShapeDtypeStruct((merged_rows, feature_width), jnp.bfloat16)
    names = jax.ShapeDtypeStruct((size, 1, src_rows), jnp.int32)
    result = jax.ShapeDtypeStruct((src_rows, feature_width), jnp.bfloat16)
    front_scratch = [
        pltpu.VMEM((chunks, size, src_rows, LANES), jnp.bfloat16),
        pltpu.VMEM((chunks, size, src_rows, LANES), jnp.bfloat16),
        pltpu.VMEM((size, 1, src_rows), jnp.int32),
        pltpu.VMEM(marks_shape, jnp.bfloat16),
        pltpu.VMEM(marks_shape, jnp.bfloat16),
        pltpu.VMEM((chunks, length, rows, LANES), jnp.float32),
        pltpu.VMEM((chunks, length + 1, rows, LANES), jnp.float32),
        pltpu.VMEM((chunks, 2, rows, LANES), jnp.float32),
        pltpu.VMEM((size * chunks, merged_rows, LANES), jnp.float32),
        dma((turns,)),
        dma((turns,)),
        dma(()),
        dma(()),
        dma((chunks, turns)),
        dma((chunks, turns)),
        dma((chunks,)),
        dma((chunks, 2)),
        dma((chunks,)),
        dma((chunks, length + 1, wide)),
        dma((chunks, length + 1, wide)),
        dma((chunks, 2, wide)),
        dma((chunks, 2, wide)),
        dma((chunks, spots)),
        dma((chunks, spots)),
        dma((chunks, spots)),
        dma((chunks, spots)),
        pltpu.SemaphoreType.REGULAR,
    ]
    rest_scratch = [
        pltpu.VMEM((heads, feature_width, 2 * HDIM), jnp.bfloat16),
        pltpu.VMEM((feature_width, inner), jnp.bfloat16),
        pltpu.VMEM((inner, feature_width), jnp.bfloat16),
        pltpu.VMEM((heads, seq_count, 2, merged_rows, HDIM), jnp.bfloat16),
        pltpu.VMEM((heads, merged_rows, HDIM), jnp.bfloat16),
        pltpu.VMEM((labels, length * rows), jnp.bfloat16),
        pltpu.VMEM((spots, merged_rows, width), jnp.float32),
        pltpu.VMEM((spots, merged_rows, width), jnp.float32),
        pltpu.VMEM((spots, merged_rows, width), jnp.float32),
        pltpu.VMEM((chunks, spots, merged_rows, LANES), jnp.bfloat16),
        pltpu.VMEM((chunks, spots, merged_rows, LANES), jnp.bfloat16),
        pltpu.VMEM((chunks, length, rows, LANES), jnp.bfloat16),
        pltpu.VMEM((chunks, size, src_rows, LANES), jnp.bfloat16),
        dma((heads + 1, 2)),
        dma((2, 2, heads, half)),
        dma((2, 2, heads, half)),
        dma((spots,)),
        dma((spots,)),
        dma((chunks, spots)),
        dma((chunks, spots)),
        dma((chunks, length)),
        dma((chunks, length)),
        dma((chunks, length)),
        dma((chunks, length)),
        dma((chunks, turns)),
        dma((chunks, turns)),
        dma((chunks,)),
    ]
    front_body = functools.partial(front_kernel, seq_count, head_count, chunks, cached)
    rest_body = functools.partial(rest_kernel, seq_count, head_count, chunks, heads)

    def call(name, number, body, out_shape, in_specs, scratch, arguments):
        return pl.pallas_call(
            body, out_shape=out_shape, in_specs=in_specs,
            out_specs=ANY if out_shape is result else [VMEM] * len(out_shape), scratch_shapes=scratch,
            compiler_params=pltpu.CompilerParams(
                collective_id=number, has_side_effects=True, vmem_limit_bytes=60 * 2**20
            ),
            name=name,
        )(*arguments)

    fused = length * rows * labels <= 2 * 2**20
    if not fused:
        made, ids = call("front", 0, front_body, [normed, names], [ANY] + [VMEM] * 4, front_scratch,
                         (tokens, owners, slots, norm_gain, norm_shift))
        return call("rest", 1, rest_body, result, [VMEM, ANY, ANY] + [VMEM] * 4, rest_scratch,
                    (made, w_qkv, w_out, query_gain, key_gain, out_gate, ids))

    def whole_kernel(*refs):
        front_in, rest_in, out = refs[:5], refs[5:10], refs[10]
        made, ids = refs[11:13]
        front_refs = refs[13:13 + len(front_scratch)]
        rest_refs = refs[13 + len(front_scratch):]
        loads, load_query, load_last = weight_loads(heads, *rest_in[:2], *rest_refs[:3], rest_refs[13])

        def start_loads():
            for load in loads + [load_query, load_last]:
                load.start()

        front_body(*front_in, made, ids, *front_refs, early=start_loads)
        rest_body(made, *rest_in, ids, out, *rest_refs, fused=True)

    kept = [pltpu.VMEM(normed.shape, normed.dtype), pltpu.VMEM(names.shape, names.dtype)]
    return call("sublayer", 2, whole_kernel, result, [ANY] + [VMEM] * 4 + [ANY] * 2 + [VMEM] * 3,
                kept + front_scratch + rest_scratch,
                (tokens, owners, slots, norm_gain, norm_shift, w_qkv, w_out, query_gain, key_gain,
                 out_gate))


def on_device(
    tokens,
    owner_shard,
    dest_slot,
    w_qkv,
    w_out,
    norm_gain,
    norm_shift,
    query_gain,
    key_gain,
    out_gate,
):
    return sublayer(tokens, owner_shard.T, dest_slot[None], jnp.transpose(w_qkv, (1, 0, 2)), w_out,
                    norm_gain[None], norm_shift[None], query_gain[None], key_gain[None], out_gate[None])


def solution(mesh):
    placed = (
        P(("seq", "head"), None),
        P(("seq", "head"), None),
        P(("seq", "head")),
        P(None, None, "head"),
        P("head", None),
        P(),
        P(),
        P(),
        P(),
        P(),
    )
    return jax.shard_map(
        on_device, mesh=mesh, in_specs=placed, out_specs=P(("seq", "head"), None), check_vma=False
    )
```
